512 devices in a mesh: grp: 16 (over z), cube: 32 (over y, x, core).
Axes of the slice: x: 4, y: 4, z: 16, core: 2. Of those that a mesh axis runs over, the one named last changes fastest.
Arguments:
- density: float32 [16, 32, 64, 512], P('grp', 'cube'), may hold values from 0.5 to 2
- momentum: float32 [16, 32, 3, 64, 512], P('grp', 'cube'), may hold values from -3 to 3
- element_size: float32 [16, 32, 3, 64], P('grp', 'cube'), may hold values from 0.5 to 2
- section_slots: int32 [16, 32, 5, 1024], P('grp', 'cube'), may hold values from 0 to 28671, as said below
- section_counts: int32 [16, 32, 5], P('grp', 'cube'), may hold values from 512 to 1024, as said below
- cross_slots: int32 [16, 32, 2, 1024], P('grp', 'cube'), may hold values from 0 to 28671, as said below
- cross_counts: int32 [16, 32, 2], P('grp', 'cube'), may hold values from 512 to 1024, as said below
Outputs:
- new_density: float32 [16, 32, 64, 512], P('grp', 'cube')
- new_momentum: float32 [16, 32, 3, 64, 512], P('grp', 'cube')
The draws below stay inside these ranges and needn't reach their ends.
Inputs may be any that keep to these rules, and one draw needn't show every extreme that they name: All slots of a device, of section_slots and cross_slots together, name different nodes. `section_counts`: the two devices of a pair have the same count for that bit; some pair fills all 1024 slots. All slots of a device, of section_slots and cross_slots together, name different nodes. `cross_counts`: a device's count toward the upper group equals the upper device's count toward the lower group; some pair fills all 1024 slots.
All inputs are finite; a program needn't handle non-finite values.
Results may differ from the reference program's by a relative error of at most 0.0003.
Values sent between devices are 32-bit elements; how exact they have to be, the bound alone decides.
No kernel may reach another device: no remote copies, remote signals or barrier semaphores. Data moves between devices by JAX's collectives and lax.ppermute only.
A program may use at most 64 MiB of HBM per device.

```python
import math
import jax
import jax.numpy as jnp
import numpy as np
from jax import lax

NODES_EL = 512
E_DEV = 64
NL = 28672
SECTIONS = 5
PS = 1024
PX = 1024
N_GRP = 16
N_CUBE = 32


def node_orders(key, salt):
    keys = jax.random.split(jax.random.fold_in(key, salt), N_GRP * N_CUBE)
    orders = jax.vmap(lambda k: jax.random.permutation(k, NL))(keys)
    return orders.reshape(N_GRP, N_CUBE, NL).astype(jnp.int32)


def draw_section_slots(key, part):
    orders = node_orders(key, 11)
    return orders[:, :, :SECTIONS * PS].reshape(N_GRP, N_CUBE, SECTIONS, PS)


def draw_cross_slots(key, part):
    orders = node_orders(key, 11)
    return orders[:, :, SECTIONS * PS:SECTIONS * PS + 2 * PX].reshape(N_GRP, N_CUBE, 2, PX)


def draw_section_counts(key, part):
    raw_counts = jax.random.randint(jax.random.fold_in(key, 21), (N_GRP, N_CUBE, SECTIONS), PS // 2, PS + 1, dtype=jnp.int32)
    raw_counts = raw_counts.at[0, 0, :].set(PS)
    member = jnp.arange(N_CUBE, dtype=jnp.int32)[:, None]
    section_ids = jnp.arange(SECTIONS, dtype=jnp.int32)[None]
    base = member - jnp.bitwise_and(member, jnp.left_shift(jnp.ones_like(section_ids), section_ids))
    return raw_counts[:, base, jnp.broadcast_to(section_ids, base.shape)].astype(jnp.int32)


def draw_cross_counts(key, part):
    raw_counts = jax.random.randint(jax.random.fold_in(key, 41), (N_GRP, N_CUBE), PX // 2, PX + 1, dtype=jnp.int32)
    raw_counts = raw_counts.at[0, 0].set(PX)
    from_lower = jnp.roll(raw_counts, 1, axis=0)
    return jnp.stack([from_lower, raw_counts], axis=-1).astype(jnp.int32)


def steps_of(stream_key, shape, shards, smallest, top_value):
    factor_of = 1.0
    for axis_at, parts in shards:
        steps = jax.random.uniform(jax.random.fold_in(jax.random.fold_in(stream_key, 6), axis_at), (parts,), jnp.float32, smallest / len(shards), top_value / len(shards))
        factor_of = factor_of * jnp.repeat(jnp.exp(steps), shape[axis_at] // parts).reshape((-1,) + (1,) * (len(shape) - 1 - axis_at))
    return factor_of


def scatter_about(key, extent, spread, bound, shards=(), kind=jnp.bfloat16):
    level = steps_of(key, extent, shards, -0.22, 0.18) if shards else 1.0
    values = jax.random.normal(key, extent, jnp.float32) * spread * level
    return jnp.minimum(jnp.maximum(values, -bound), bound).astype(kind)


def setup_inputs(seed: int = 0) -> dict:
    key_list = jax.random.split(jax.random.key(seed), 8)
    density = jnp.clip(jnp.exp(math.log(2.0) - 1.3862944 * jax.random.uniform(key_list[0], (N_GRP, N_CUBE, E_DEV, NODES_EL), jnp.float32) ** steps_of(key_list[0], (N_GRP, N_CUBE, E_DEV, NODES_EL), ((0, 16), (1, 32)), -0.2, 0.2)), 0.5, 2.0)
    momentum = scatter_about(key_list[1], (N_GRP, N_CUBE, 3, E_DEV, NODES_EL), 0.5, 3.0, ((0, 16), (1, 32)), jnp.float32)
    element_size = jnp.clip(jnp.exp(math.log(2.0) - 1.3862944 * jax.random.uniform(key_list[2], (N_GRP, N_CUBE, 3, E_DEV), jnp.float32) ** steps_of(key_list[2], (N_GRP, N_CUBE, 3, E_DEV), ((0, 16), (1, 32)), -0.2, 0.2)), 0.5, 2.0)
    section_slots = draw_section_slots(jax.random.fold_in(key_list[7], 71), 0)
    section_counts = draw_section_counts(jax.random.fold_in(key_list[7], 71), 0)
    cross_slots = draw_cross_slots(jax.random.fold_in(key_list[7], 71), 0)
    cross_counts = draw_cross_counts(jax.random.fold_in(key_list[7], 71), 0)
    return {"density": density, "momentum": momentum, "element_size": element_size, "section_slots": section_slots, "section_counts": section_counts, "cross_slots": cross_slots, "cross_counts": cross_counts}


GAMMA = 1.4
DT = 0.01
ORDER = 7


def gll_tables():
    points = np.array([-1.0, -0.8717401485096066, -0.5917001814331423, -0.2092992179024789, 0.2092992179024789, 0.5917001814331423, 0.8717401485096066, 1.0])
    weights = np.array([1.0 / 28.0, 0.2107042271435061, 0.3411226924835044, 0.4124587946587038, 0.4124587946587038, 0.3411226924835044, 0.2107042271435061, 1.0 / 28.0])
    previous = np.ones(8)
    current = points.copy()
    for order_now in range(1, ORDER):
        following = ((2 * order_now + 1) * points * current - order_now * previous) / (order_now + 1)
        previous = current
        current = following
    derivative = np.zeros((8, 8))
    for i in range(8):
        for j in range(8):
            if i != j:
                derivative[i, j] = current[i] / (current[j] * (points[i] - points[j]))
    derivative[0, 0] = -ORDER * (ORDER + 1) / 4.0
    derivative[7, 7] = ORDER * (ORDER + 1) / 4.0
    return points, weights, derivative


def node_map(elements):
    element_ids = jnp.arange(elements, dtype=jnp.int32)[:, None]
    node_ids = jnp.arange(512, dtype=jnp.int32)[None]
    slab = (7 * element_ids + node_ids // 64) % (7 * elements)
    return (slab * 64 + node_ids % 64).astype(jnp.int32)


def local_sums(density, momentum, element_size):
    points, weights, derivative = gll_tables()
    deriv_table = jnp.asarray(derivative, jnp.float32)
    elements = density.shape[0]
    element_nodes = node_map(elements)
    velocity = momentum / density[None]
    pressure = jnp.exp(GAMMA * jnp.log(density))
    scales = 2.0 / element_size

    def along_axis(fluxes, axis_num):
        shaped = fluxes.reshape(elements, 8, 8, 8)
        if axis_num == 0:
            result = jnp.einsum('ai,eijk->eajk', deriv_table, shaped, precision=lax.Precision.HIGHEST)
        elif axis_num == 1:
            result = jnp.einsum('aj,eijk->eiak', deriv_table, shaped, precision=lax.Precision.HIGHEST)
        else:
            result = jnp.einsum('ak,eijk->eija', deriv_table, shaped, precision=lax.Precision.HIGHEST)
        return result.reshape(elements, 512) * scales[axis_num][:, None]

    residuals = []
    for component in range(4):
        totals = jnp.zeros_like(density)
        for axis_num in range(3):
            if component == 0:
                fluxes = momentum[axis_num]
            else:
                fluxes = momentum[component - 1] * velocity[axis_num]
                if component - 1 == axis_num:
                    fluxes = fluxes + pressure
            totals = totals - along_axis(fluxes, axis_num)
        residuals.append(totals)
    node_weight = jnp.asarray(np.kron(weights, np.kron(weights, weights)), jnp.float32)
    jacobian = element_size[0] * element_size[1] * element_size[2] / 8.0
    weight = jacobian[:, None] * node_weight[None]
    values = jnp.stack([part * weight for part in residuals] + [weight])
    return jnp.zeros((5, NL), jnp.float32).at[:, element_nodes.reshape(-1)].add(values.reshape(5, -1))


def pick_slots(sums, slots, counts):
    live_mask = (jnp.arange(slots.shape[-1])[None] < counts[:, None]).astype(jnp.float32)
    return sums[:, slots] * live_mask[None]


def combine(sums, section_in, section_ids, cross_in, cross_ids):
    all_slots = jnp.concatenate([section_ids.reshape(-1), cross_ids.reshape(-1)])
    incoming = jnp.concatenate([section_in.reshape(5, -1), cross_in.reshape(5, -1)], axis=1)
    totals = sums.at[:, all_slots].add(incoming)
    return totals[:4] / totals[4:]


def update(density, momentum, assembled):
    element_nodes = node_map(density.shape[0])
    at_nodes = assembled[:, element_nodes]
    return density + DT * at_nodes[0], momentum + DT * at_nodes[1:]


def reference(density, momentum, element_size, section_slots, section_counts, cross_slots, cross_counts):
    def group_sums(pieces):
        return jax.vmap(local_sums)(*pieces)

    sums = lax.map(group_sums, (density, momentum, element_size))
    pick_all = jax.vmap(jax.vmap(pick_slots))
    section_send = pick_all(sums, section_slots, section_counts)
    cross_send = pick_all(sums, cross_slots, cross_counts)
    member = jnp.arange(N_CUBE)
    received = []
    for b in range(SECTIONS):
        partner = jnp.bitwise_xor(member, 1 << b)
        received.append(section_send[:, :, :, b][:, partner])
    section_recv = jnp.stack(received, axis=3)
    from_lower = jnp.roll(cross_send[:, :, :, 1], 1, axis=0)
    from_upper = jnp.roll(cross_send[:, :, :, 0], -1, axis=0)
    cross_recv = jnp.stack([from_lower, from_upper], axis=3)
    assembled = jax.vmap(jax.vmap(combine))(sums, section_recv, section_slots, cross_recv, cross_slots)
    new_density, new_momentum = jax.vmap(jax.vmap(update))(density, momentum, assembled)
    return new_density, new_momentum
```

```python
import jax
import jax.numpy as jnp
import numpy as np
from jax import lax
from jax.experimental import pallas as pl
from jax.experimental.pallas import tpu as pltpu
from jax.sharding import PartitionSpec as P

GAMMA = 1.4
DT = 0.01
ORDER = 7
COLS = 448
F32 = jnp.float32
BF16 = jnp.bfloat16


def gll_tables():
    points = np.array(
        [
            -1.0,
            -0.8717401485096066,
            -0.5917001814331423,
            -0.2092992179024789,
            0.2092992179024789,
            0.5917001814331423,
            0.8717401485096066,
            1.0,
        ]
    )
    weights = np.array(
        [
            1.0 / 28.0,
            0.2107042271435061,
            0.3411226924835044,
            0.4124587946587038,
            0.4124587946587038,
            0.3411226924835044,
            0.2107042271435061,
            1.0 / 28.0,
        ]
    )
    previous = np.ones(8)
    current = points.copy()
    for order_now in range(1, ORDER):
        following = ((2 * order_now + 1) * points * current - order_now * previous) / (
            order_now + 1
        )
        previous = current
        current = following
    derivative = np.zeros((8, 8))
    for i in range(8):
        for j in range(8):
            if i != j:
                derivative[i, j] = current[i] / (current[j] * (points[i] - points[j]))
    derivative[0, 0] = -ORDER * (ORDER + 1) / 4.0
    derivative[7, 7] = ORDER * (ORDER + 1) / 4.0
    return (points, weights, derivative)


def bf16_parts(table, count):
    rest = np.asarray(table, np.float32)
    parts = []
    for _ in range(count):
        part = rest.astype(BF16)
        parts.append(part)
        rest = rest - part.astype(np.float32)
    return parts


def tables():
    _, weights, derivative = gll_tables()
    along_first = np.kron(derivative, np.eye(64)).T
    along_second = np.kron(np.eye(4), np.kron(derivative, np.eye(8))).T
    along_third = np.kron(np.eye(32), derivative).T
    first = np.stack(bf16_parts(along_first, 2))
    inner = np.stack(bf16_parts(along_second, 2) + bf16_parts(along_third, 2))
    node = np.kron(weights, np.kron(weights, weights)).astype(np.float32)[None]
    node_parts = np.concatenate(
        bf16_parts(node, 3) + [np.zeros((13, 512), np.float32).astype(BF16)], axis=0
    )
    return first, inner, node, node_parts


def split(value):
    high = value.astype(BF16)
    low = (value - high.astype(F32)).astype(BF16)
    return high, low


def element_and_column(ids):
    element = lax.shift_right_logical(lax.shift_right_logical(ids, 6) * 9363, 16)
    return element, ids - element * COLS


def column_onehot(column):
    rows = lax.broadcasted_iota(jnp.int32, (512, column.shape[1]), 0)
    return jnp.where(rows == column, 1.0, 0.0).astype(BF16)


def element_mask(element):
    rows = lax.broadcasted_iota(jnp.int32, (64, element.shape[1]), 0)
    return rows == element


def as_column(row):
    shape = (64, 64)
    same = lax.broadcasted_iota(jnp.int32, shape, 0) == lax.broadcasted_iota(jnp.int32, shape, 1)
    return jnp.sum(jnp.where(same, row, 0.0), axis=1, keepdims=True)


def low_lanes(shape):
    return lax.broadcasted_iota(jnp.int32, shape, 1) < 64


def sums_kernel(
    density, momentum, sizes, first, inner, node, node_parts, section, cross, section_n, cross_n,
    sums, *sends_and_scratch,
):
    sends, (table,) = sends_and_scratch[:7], sends_and_scratch[7:]
    rho = density[...]
    inverse = 1.0 / rho
    mom = [momentum[a] for a in range(3)]
    velocity = [m * inverse for m in mom]
    pressure = jnp.exp(GAMMA * jnp.log(rho))
    h = [as_column(sizes[d : d + 1, :]) for d in range(3)]
    scale = [h[1] * h[2] * 0.25, h[0] * h[2] * 0.25, h[0] * h[1] * 0.25]
    jacobian = h[0] * h[1] * h[2] * 0.125

    def flux(d):
        parts = [mom[d]]
        for a in range(3):
            part = mom[a] * velocity[d]
            parts.append(part + pressure if a == d else part)
        return split(jnp.concatenate([part * scale[d] for part in parts], axis=0))

    def dot(a, b):
        return jnp.dot(a, b, preferred_element_type=F32)

    high, low = flux(0)
    change = dot(high, first[0]) + dot(low, first[0]) + dot(high, first[1])
    halves = [change[:, :256], change[:, 256:]]
    for d in (1, 2):
        high, low = flux(d)
        big, small = inner[2 * d - 2], inner[2 * d - 1]
        for k in range(2):
            lanes = slice(256 * k, 256 * k + 256)
            halves[k] += dot(high[:, lanes], big) + dot(low[:, lanes], big)
            halves[k] += dot(high[:, lanes], small)
    change = jnp.concatenate(halves, axis=1)
    node_w = node[...]
    for f in range(5):
        value = -change[64 * f : 64 * f + 64] * node_w if f < 4 else jacobian * node_w
        face = pltpu.roll(pltpu.roll(value[:, 384:], 64, 1), 1, 0)
        head = value[:, :128] + jnp.where(low_lanes((64, 128)), face, 0.0)
        value = jnp.concatenate([head, value[:, 128:]], axis=1)
        sums[f] = value
        if f < 4:
            high, low = split(value)
            table[64 * f : 64 * f + 64, :] = high
            table[64 * f + 256 : 64 * f + 320, :] = low
    table[512:528, :] = node_parts[...]
    before = pltpu.roll(jnp.broadcast_to(jacobian, (64, 128)), 1, 0)[:, :1]

    for s in range(7):
        ids, count = (section[s : s + 1, :], section_n[s]) if s < 5 else (
            cross[s - 5 : s - 4, :], cross_n[s - 5])
        element, column = element_and_column(ids)
        picked = dot(table[...], column_onehot(column))
        mask = element_mask(element)
        live = lax.broadcasted_iota(jnp.int32, ids.shape, 1) < count
        for f in range(4):
            row = picked[64 * f : 64 * f + 64] + picked[64 * f + 256 : 64 * f + 320]
            row = jnp.sum(jnp.where(mask, row, 0.0), axis=0, keepdims=True)
            sends[s][f : f + 1, :] = jnp.where(live, row, 0.0)
        volume = jnp.where(mask, jacobian, 0.0)
        face_volume = jnp.where(jnp.logical_and(mask, column < 64), before, 0.0)
        volume = jnp.sum(volume + face_volume, axis=0, keepdims=True)
        at_column = picked[512:513] + picked[513:514] + picked[514:515]
        sends[s][4:5, :] = jnp.where(live, volume * at_column, 0.0)


def update_kernel(
    density, momentum, sums, section, cross, *received_and_outputs,
):
    received = received_and_outputs[:7]
    new_density, new_momentum, total = received_and_outputs[7:]
    for s in range(7):
        ids = section[s : s + 1, :] if s < 5 else cross[s - 5 : s - 4, :]
        element, column = element_and_column(ids)
        onehot = column_onehot(column)
        mask = element_mask(element)
        high, low = split(received[s][...])
        rows = []
        for part in (high, low):
            for f in range(5):
                rows.append(jnp.where(mask, part[f : f + 1, :].astype(F32), 0.0).astype(BF16))
        added = lax.dot_general(
            jnp.concatenate(rows, axis=0), onehot, (((1,), (1,)), ((), ())),
            preferred_element_type=F32,
        )
        added = added[:320] + added[320:]
        if s == 0:
            total[...] = added
        else:
            total[...] += added
    lanes = lax.broadcasted_iota(jnp.int32, (64, 128), 1)
    weight = sums[4] + total[256:320]
    share = DT / weight
    for f in range(4):
        step = (sums[f] + total[64 * f : 64 * f + 64]) * share
        face = pltpu.roll(pltpu.roll(step[:, :128], 64, 1), 63, 0)
        tail = jnp.where(lanes < 64, step[:, 384:], face)
        step = jnp.concatenate([step[:, :384], tail], axis=1)
        if f == 0:
            new_density[...] = density[...] + step
        else:
            new_momentum[f - 1] = momentum[f - 1] + step


def local(
    density, momentum, element_size, section_slots, section_counts, cross_slots, cross_counts
):
    rho, mom, sizes = density[0, 0], momentum[0, 0], element_size[0, 0]
    section, cross = section_slots[0, 0], cross_slots[0, 0]
    slots = section.shape[1]
    whole = pl.BlockSpec(memory_space=pltpu.VMEM)
    scalars = pl.BlockSpec(memory_space=pltpu.SMEM)
    sent = jax.ShapeDtypeStruct((5, slots), F32)
    sums, *sends = pl.pallas_call(
        sums_kernel,
        out_shape=(jax.ShapeDtypeStruct((5, 64, 512), F32),) + (sent,) * 7,
        in_specs=[whole] * 9 + [scalars] * 2,
        out_specs=(whole,) * 8,
        scratch_shapes=[pltpu.VMEM((528, 512), BF16)],
        name="sums_and_gather",
    )(
        rho, mom, sizes, *[jnp.asarray(t) for t in tables()], section, cross,
        section_counts[0, 0], cross_counts[0, 0],
    )
    members = lax.axis_size("cube")
    groups = lax.axis_size("grp")
    received = [
        lax.ppermute(sends[b], "cube", [(i, i ^ (1 << b)) for i in range(members)])
        for b in range(5)
    ]
    received.append(
        lax.ppermute(sends[6], "grp", [(i, (i + 1) % groups) for i in range(groups)])
    )
    received.append(
        lax.ppermute(sends[5], "grp", [((i + 1) % groups, i) for i in range(groups)])
    )
    new_density, new_momentum = pl.pallas_call(
        update_kernel,
        out_shape=(
            jax.ShapeDtypeStruct(rho.shape, F32),
            jax.ShapeDtypeStruct(mom.shape, F32),
        ),
        in_specs=[whole] * 12,
        out_specs=(whole,) * 2,
        scratch_shapes=[pltpu.VMEM((320, 512), F32)],
        name="scatter_and_update",
    )(rho, mom, sums, section, cross, *received)
    return (new_density[None, None], new_momentum[None, None])


def solution(mesh):
    placed = (
        P("grp", "cube", None, None),
        P("grp", "cube", None, None, None),
        P("grp", "cube", None, None),
        P("grp", "cube", None, None),
        P("grp", "cube", None),
        P("grp", "cube", None, None),
        P("grp", "cube", None),
    )
    return jax.shard_map(
        local,
        mesh=mesh,
        in_specs=placed,
        out_specs=(P("grp", "cube", None, None), P("grp", "cube", None, None, None)),
        check_vma=False,
    )
```

```python
import jax
import jax.numpy as jnp
import numpy as np
from jax import lax
from jax.experimental import pallas as pl
from jax.experimental.pallas import tpu as pltpu
from jax.sharding import PartitionSpec as P

GAMMA = 1.4
DT = 0.01
ORDER = 7
COLS = 448
F32 = jnp.float32
BF16 = jnp.bfloat16


def gll_tables():
    points = np.array(
        [
            -1.0,
            -0.8717401485096066,
            -0.5917001814331423,
            -0.2092992179024789,
            0.2092992179024789,
            0.5917001814331423,
            0.8717401485096066,
            1.0,
        ]
    )
    weights = np.array(
        [
            1.0 / 28.0,
            0.2107042271435061,
            0.3411226924835044,
            0.4124587946587038,
            0.4124587946587038,
            0.3411226924835044,
            0.2107042271435061,
            1.0 / 28.0,
        ]
    )
    previous = np.ones(8)
    current = points.copy()
    for order_now in range(1, ORDER):
        following = ((2 * order_now + 1) * points * current - order_now * previous) / (
            order_now + 1
        )
        previous = current
        current = following
    derivative = np.zeros((8, 8))
    for i in range(8):
        for j in range(8):
            if i != j:
                derivative[i, j] = current[i] / (current[j] * (points[i] - points[j]))
    derivative[0, 0] = -ORDER * (ORDER + 1) / 4.0
    derivative[7, 7] = ORDER * (ORDER + 1) / 4.0
    return (points, weights, derivative)


def bf16_parts(table, count):
    rest = np.asarray(table, np.float32)
    parts = []
    for _ in range(count):
        part = rest.astype(BF16)
        parts.append(part)
        rest = rest - part.astype(np.float32)
    return parts


def tables():
    _, weights, derivative = gll_tables()
    along_first = np.kron(derivative, np.eye(64)).T
    along_second = np.kron(np.eye(4), np.kron(derivative, np.eye(8))).T
    along_third = np.kron(np.eye(32), derivative).T
    first = np.stack(bf16_parts(along_first, 2))
    inner = np.stack(bf16_parts(along_second, 2) + bf16_parts(along_third, 2))
    node = np.kron(weights, np.kron(weights, weights)).astype(np.float32)[None]
    node_parts = np.concatenate(
        bf16_parts(node, 3) + [np.zeros((13, 512), np.float32).astype(BF16)], axis=0
    )
    return first, inner, node, node_parts


def split(value):
    high = value.astype(BF16)
    low = (value - high.astype(F32)).astype(BF16)
    return high, low


def element_and_column(ids):
    element = lax.shift_right_logical(lax.shift_right_logical(ids, 6) * 9363, 16)
    return element, ids - element * COLS


def column_onehot(column):
    rows = lax.broadcasted_iota(jnp.int32, (512, column.shape[1]), 0)
    return jnp.where(rows == column, 1.0, 0.0).astype(BF16)


def element_mask(element):
    rows = lax.broadcasted_iota(jnp.int32, (64, element.shape[1]), 0)
    return rows == element


def as_column(row):
    shape = (64, 64)
    same = lax.broadcasted_iota(jnp.int32, shape, 0) == lax.broadcasted_iota(jnp.int32, shape, 1)
    return jnp.sum(jnp.where(same, row, 0.0), axis=1, keepdims=True)


def low_lanes(shape):
    return lax.broadcasted_iota(jnp.int32, shape, 1) < 64


def dot(a, b):
    return jnp.dot(a, b, preferred_element_type=F32)


def pick(table, volumes, ids, count, send, at):
    element, column = element_and_column(ids)
    picked = dot(table[...], column_onehot(column))
    mask = element_mask(element)
    live = lax.broadcasted_iota(jnp.int32, ids.shape, 1) < count
    volume = jnp.where(mask, volumes[0, :, :1], 0.0)
    face_volume = jnp.where(jnp.logical_and(mask, column < 64), volumes[1, :, :1], 0.0)
    volume = jnp.sum(volume + face_volume, axis=0, keepdims=True)
    rows = []
    for f in range(4):
        row = picked[64 * f : 64 * f + 64] + picked[64 * f + 256 : 64 * f + 320]
        rows.append(jnp.sum(jnp.where(mask, row, 0.0), axis=0, keepdims=True))
    rows.append(volume * (picked[512:513] + picked[513:514] + picked[514:515]))
    for f in range(5):
        row = jnp.where(live, rows[f], 0.0)
        for t in range(8):
            send[at, f, t : t + 1, :] = row[:, 128 * t : 128 * t + 128]


def spread(ids, values):
    element, column = element_and_column(ids)
    mask = element_mask(element)
    rows = []
    for f in range(5):
        row = jnp.concatenate([values[f, t : t + 1, :] for t in range(8)], axis=1)
        rows.append(split(row))
    rows = [jnp.where(mask, row[p].astype(F32), 0.0).astype(BF16) for p in (0, 1) for row in rows]
    added = lax.dot_general(
        jnp.concatenate(rows, axis=0), column_onehot(column), (((1,), (1,)), ((), ())),
        preferred_element_type=F32,
    )
    return added[:320] + added[320:]


def carried(side, section, cross, arriving):
    lower = side == (0 if arriving else 1)
    return [
        section[2 + 2 * side],
        section[1 + 2 * side],
        jnp.where(lower, cross[0:1, :], cross[1:2, :]),
    ]


def carried_counts(side, section_n, cross_n):
    return [section_n[2 + 2 * side], section_n[1 + 2 * side], cross_n[1 - side]]


def sums_kernel(
    density, momentum, sizes, first, inner, node, node_parts, section, cross, section_n, cross_n,
    core, sums, table, volumes, send,
):
    rho = density[...]
    inverse = 1.0 / rho
    mom = [momentum[a] for a in range(3)]
    velocity = [m * inverse for m in mom]
    pressure = jnp.exp(GAMMA * jnp.log(rho))
    h = [as_column(sizes[d]) for d in range(3)]
    scale = [h[1] * h[2] * 0.25, h[0] * h[2] * 0.25, h[0] * h[1] * 0.25]
    jacobian = h[0] * h[1] * h[2] * 0.125

    def flux(d):
        parts = [mom[d]]
        for a in range(3):
            part = mom[a] * velocity[d]
            parts.append(part + pressure if a == d else part)
        return split(jnp.concatenate([part * scale[d] for part in parts], axis=0))

    high, low = flux(0)
    change = dot(high, first[0]) + dot(low, first[0]) + dot(high, first[1])
    halves = [change[:, :256], change[:, 256:]]
    for d in (1, 2):
        high, low = flux(d)
        big, small = inner[2 * d - 2], inner[2 * d - 1]
        for k in range(2):
            lanes = slice(256 * k, 256 * k + 256)
            halves[k] += dot(high[:, lanes], big) + dot(low[:, lanes], big)
            halves[k] += dot(high[:, lanes], small)
    change = jnp.concatenate(halves, axis=1)
    node_w = node[...]
    for f in range(5):
        value = -change[64 * f : 64 * f + 64] * node_w if f < 4 else jacobian * node_w
        face = pltpu.roll(pltpu.roll(value[:, 384:], 64, 1), 1, 0)
        head = value[:, :128] + jnp.where(low_lanes((64, 128)), face, 0.0)
        value = jnp.concatenate([head, value[:, 128:]], axis=1)
        sums[f] = value
        if f < 4:
            high, low = split(value)
            table[64 * f : 64 * f + 64, :] = high
            table[64 * f + 256 : 64 * f + 320, :] = low
    table[512:528, :] = node_parts[...]
    volumes[0] = jnp.broadcast_to(jacobian, (64, 128))
    volumes[1] = pltpu.roll(volumes[0], 1, 0)

    pick(table, volumes, section[0], section_n[0], send, 0)
    ids = carried(1 - core[0], section, cross, False)
    counts = carried_counts(1 - core[0], section_n, cross_n)
    for j in range(3):
        pick(table, volumes, ids[j], counts[j], send, j + 1)


def gather_kernel(table, volumes, section, cross, section_n, cross_n, core, send):
    ids = carried(core[0], section, cross, False)
    counts = carried_counts(core[0], section_n, cross_n)
    for j in range(3):
        pick(table, volumes, ids[j], counts[j], send, j)


def pack_kernel(far_a, far_b, far_c, back):
    for j, far in enumerate((far_a, far_b, far_c)):
        back[j] = far[1]


def scatter_kernel(
    sums, section, cross, core, shared, far_a, far_b, far_c, total
):
    added = spread(section[0], shared[0])
    ids = carried(core[0], section, cross, True)
    for j, far in enumerate((far_a, far_b, far_c)):
        added += spread(ids[j], far[0])
    for f in range(5):
        total[f] = sums[f] + added[64 * f : 64 * f + 64]


def update_kernel(
    density, momentum, total, section, cross, core, relayed,
    new_density, new_momentum,
):
    ids = carried(1 - core[0], section, cross, True)
    added = spread(ids[0], relayed[0]) + spread(ids[1], relayed[1]) + spread(ids[2], relayed[2])
    lanes = lax.broadcasted_iota(jnp.int32, (64, 128), 1)
    share = DT / (total[4] + added[256:320])
    for f in range(4):
        step = (total[f] + added[64 * f : 64 * f + 64]) * share
        face = pltpu.roll(pltpu.roll(step[:, :128], 64, 1), 63, 0)
        tail = jnp.where(lanes < 64, step[:, 384:], face)
        step = jnp.concatenate([step[:, :384], tail], axis=1)
        if f == 0:
            new_density[...] = density[...] + step
        else:
            new_momentum[f - 1] = momentum[f - 1] + step


def relay_pairs(mesh_shape, step):
    groups, members = mesh_shape
    pairs = []
    for g in range(groups):
        for m in range(members):
            core = m % 2
            if step < 2:
                target = (g, m ^ (1 << (2 - step + 2 * core)))
            else:
                target = ((g + 1 - 2 * core) % groups, m)
            pairs.append((g * members + m, target[0] * members + target[1]))
    return pairs


def local(
    density, momentum, element_size, section_slots, section_counts, cross_slots, cross_counts
):
    rho, mom = density[0, 0], momentum[0, 0]
    sizes = element_size.reshape(3, 1, 64)
    slots = section_slots.shape[-1]
    section = section_slots.reshape(5, 1, slots)
    cross = cross_slots[0, 0]
    core = (lax.axis_index("cube") & 1).reshape(1)
    where = (section, cross, section_counts[0, 0], cross_counts[0, 0], core)
    whole = pl.BlockSpec(memory_space=pltpu.VMEM)
    scalars = pl.BlockSpec(memory_space=pltpu.SMEM)
    where_specs = [whole] * 2 + [scalars] * 3
    places = (section, cross, core)
    place_specs = [whole] * 2 + [scalars]
    members = lax.axis_size("cube")
    groups = lax.axis_size("grp")
    near = [(i, i ^ 1) for i in range(members)]

    def on_chip(value):
        return pltpu.with_memory_space_constraint(value, pltpu.VMEM)

    def near_chip(shape, dtype=F32):
        return pltpu.VMEM(shape, dtype)

    sums, table, volumes, to_other = pl.pallas_call(
        sums_kernel,
        out_shape=(
            near_chip((5, 64, 512)),
            near_chip((528, 512), BF16),
            near_chip((2, 64, 128)),
            near_chip((4, 5, 8, 128)),
        ),
        in_specs=[whole] * 7 + where_specs,
        out_specs=(whole,) * 4,
        name="sums_and_gather",
    )(rho, mom, sizes, *[jnp.asarray(t) for t in tables()], *where)
    shared = lax.ppermute(to_other, "cube", near)
    own = pl.pallas_call(
        gather_kernel,
        out_shape=near_chip((3, 5, 8, 128)),
        in_specs=[whole] * 2 + where_specs,
        out_specs=whole,
        name="gather",
    )(on_chip(table), on_chip(volumes), *where)
    far = [None] * 3
    for step in ORDER_OF_STEPS:
        both = jnp.stack([own[step], shared[step + 1]])
        far[step] = lax.ppermute(both, ("grp", "cube"), relay_pairs((groups, members), step))
    far = [on_chip(part) for part in far]
    back = pl.pallas_call(
        pack_kernel,
        out_shape=near_chip((3, 5, 8, 128)),
        in_specs=[whole] * 3,
        out_specs=whole,
        name="pack",
    )(*far)
    relayed = lax.ppermute(back, "cube", near)
    total = pl.pallas_call(
        scatter_kernel,
        out_shape=near_chip((5, 64, 512)),
        in_specs=[whole] + place_specs + [whole] * 4,
        out_specs=whole,
        name="scatter",
    )(on_chip(sums), *places, on_chip(shared), *far)
    new_density, new_momentum = pl.pallas_call(
        update_kernel,
        out_shape=(
            jax.ShapeDtypeStruct(rho.shape, F32),
            jax.ShapeDtypeStruct(mom.shape, F32),
        ),
        in_specs=[whole] * 3 + place_specs + [whole],
        out_specs=(whole,) * 2,
        name="scatter_and_update",
    )(on_chip(rho), on_chip(mom), on_chip(total), *places, on_chip(relayed))
    return (new_density[None, None], new_momentum[None, None])


ORDER_OF_STEPS = (2, 0, 1)


def solution(mesh):
    placed = (
        P("grp", "cube", None, None),
        P("grp", "cube", None, None, None),
        P("grp", "cube", None, None),
        P("grp", "cube", None, None),
        P("grp", "cube", None),
        P("grp", "cube", None, None),
        P("grp", "cube", None),
    )
    return jax.shard_map(
        local,
        mesh=mesh,
        in_specs=placed,
        out_specs=(P("grp", "cube", None, None), P("grp", "cube", None, None, None)),
        check_vma=False,
    )
```

```python
import jax
import jax.numpy as jnp
import numpy as np
from jax import lax
from jax.experimental import pallas as pl
from jax.experimental.pallas import tpu as pltpu
from jax.sharding import PartitionSpec as P

GAMMA = 1.4
DT = 0.01
ORDER = 7
COLS = 448
F32 = jnp.float32
BF16 = jnp.bfloat16


def gll_tables():
    points = np.array(
        [
            -1.0,
            -0.8717401485096066,
            -0.5917001814331423,
            -0.2092992179024789,
            0.2092992179024789,
            0.5917001814331423,
            0.8717401485096066,
            1.0,
        ]
    )
    weights = np.array(
        [
            1.0 / 28.0,
            0.2107042271435061,
            0.3411226924835044,
            0.4124587946587038,
            0.4124587946587038,
            0.3411226924835044,
            0.2107042271435061,
            1.0 / 28.0,
        ]
    )
    previous = np.ones(8)
    current = points.copy()
    for order_now in range(1, ORDER):
        following = ((2 * order_now + 1) * points * current - order_now * previous) / (
            order_now + 1
        )
        previous = current
        current = following
    derivative = np.zeros((8, 8))
    for i in range(8):
        for j in range(8):
            if i != j:
                derivative[i, j] = current[i] / (current[j] * (points[i] - points[j]))
    derivative[0, 0] = -ORDER * (ORDER + 1) / 4.0
    derivative[7, 7] = ORDER * (ORDER + 1) / 4.0
    return (points, weights, derivative)


def bf16_parts(table, count):
    rest = np.asarray(table, np.float32)
    parts = []
    for _ in range(count):
        part = rest.astype(BF16)
        parts.append(part)
        rest = rest - part.astype(np.float32)
    return parts


def tables():
    _, weights, derivative = gll_tables()
    along_first = np.kron(derivative, np.eye(64)).T
    along_second = np.kron(np.eye(4), np.kron(derivative, np.eye(8))).T
    along_third = np.kron(np.eye(32), derivative).T
    first = np.stack(bf16_parts(along_first, 2))
    inner = np.stack(bf16_parts(along_second, 2) + bf16_parts(along_third, 2))
    node = np.kron(weights, np.kron(weights, weights)).astype(np.float32)[None]
    node_parts = np.concatenate(
        bf16_parts(node, 3) + [np.zeros((13, 512), np.float32).astype(BF16)], axis=0
    )
    return first, inner, node, node_parts


def split(value):
    high = value.astype(BF16)
    low = (value - high.astype(F32)).astype(BF16)
    return high, low


def element_and_column(ids):
    element = lax.shift_right_logical(lax.shift_right_logical(ids, 6) * 9363, 16)
    return element, ids - element * COLS


def column_onehot(column):
    rows = lax.broadcasted_iota(jnp.int32, (512, column.shape[1]), 0)
    return jnp.where(rows == column, 1.0, 0.0).astype(BF16)


def element_mask(element):
    rows = lax.broadcasted_iota(jnp.int32, (64, element.shape[1]), 0)
    return rows == element


def as_column(row):
    shape = (64, 64)
    same = lax.broadcasted_iota(jnp.int32, shape, 0) == lax.broadcasted_iota(jnp.int32, shape, 1)
    return jnp.sum(jnp.where(same, row, 0.0), axis=1, keepdims=True)


def low_lanes(shape):
    return lax.broadcasted_iota(jnp.int32, shape, 1) < 64


def dot(a, b):
    return jnp.dot(a, b, preferred_element_type=F32)


def pick(table, volumes, ids, count, send, at):
    element, column = element_and_column(ids)
    picked = dot(table[...], column_onehot(column))
    mask = element_mask(element)
    live = lax.broadcasted_iota(jnp.int32, ids.shape, 1) < count
    volume = jnp.where(mask, volumes[0, :, :1], 0.0)
    face_volume = jnp.where(jnp.logical_and(mask, column < 64), volumes[1, :, :1], 0.0)
    volume = jnp.sum(volume + face_volume, axis=0, keepdims=True)
    rows = []
    for f in range(4):
        row = picked[64 * f : 64 * f + 64] + picked[64 * f + 256 : 64 * f + 320]
        rows.append(jnp.sum(jnp.where(mask, row, 0.0), axis=0, keepdims=True))
    rows.append(volume * (picked[512:513] + picked[513:514] + picked[514:515]))
    for f in range(5):
        row = jnp.where(live, rows[f], 0.0)
        for t in range(8):
            send[at, f, t : t + 1, :] = row[:, 128 * t : 128 * t + 128]


def spread(ids, count, own, got):
    at = lax.broadcasted_iota(jnp.int32, (8, 128), 0) * 128
    live = at + lax.broadcasted_iota(jnp.int32, (8, 128), 1) < count
    before = DT / own[4]
    after = DT / (own[4] + got[4])
    parts = []
    for f in range(4):
        change = (own[f] + got[f]) * after - own[f] * before
        parts.append(split(jnp.where(live, change, 0.0)))
    element, column = element_and_column(ids)
    mask = element_mask(element)
    rows = []
    for p in range(2):
        for f in range(4):
            part = parts[f][p].astype(F32)
            row = jnp.concatenate([part[t : t + 1, :] for t in range(8)], axis=1)
            rows.append(jnp.where(mask, row, 0.0).astype(BF16))
    added = lax.dot_general(
        jnp.concatenate(rows, axis=0), column_onehot(column), (((1,), (1,)), ((), ())),
        preferred_element_type=F32,
    )
    return added[:256] + added[256:]


def carried(side, section, cross, arriving):
    lower = side == (0 if arriving else 1)
    return [
        section[2 + 2 * side],
        section[1 + 2 * side],
        jnp.where(lower, cross[0:1, :], cross[1:2, :]),
    ]


def carried_counts(side, section_n, cross_n, arriving):
    lower = side == (0 if arriving else 1)
    return [
        section_n[2 + 2 * side],
        section_n[1 + 2 * side],
        jnp.where(lower, cross_n[0], cross_n[1]),
    ]


def sums_kernel(
    density, momentum, sizes, first, inner, node, node_parts, section, cross, section_n, cross_n,
    core, steps, table, volumes, send,
):
    rho = density[...]
    inverse = 1.0 / rho
    mom = [momentum[a] for a in range(3)]
    velocity = [m * inverse for m in mom]
    pressure = jnp.exp(GAMMA * jnp.log(rho))
    h = [as_column(sizes[d]) for d in range(3)]
    scale = [h[1] * h[2] * 0.25, h[0] * h[2] * 0.25, h[0] * h[1] * 0.25]
    jacobian = h[0] * h[1] * h[2] * 0.125

    def flux(d):
        parts = [mom[d]]
        for a in range(3):
            part = mom[a] * velocity[d]
            parts.append(part + pressure if a == d else part)
        return split(jnp.concatenate([part * scale[d] for part in parts], axis=0))

    high, low = flux(0)
    change = dot(high, first[0]) + dot(low, first[0]) + dot(high, first[1])
    halves = [change[:, :256], change[:, 256:]]
    for d in (1, 2):
        high, low = flux(d)
        big, small = inner[2 * d - 2], inner[2 * d - 1]
        for k in range(2):
            lanes = slice(256 * k, 256 * k + 256)
            halves[k] += dot(high[:, lanes], big) + dot(low[:, lanes], big)
            halves[k] += dot(high[:, lanes], small)
    change = jnp.concatenate(halves, axis=1)
    node_w = node[...]

    def with_face(value):
        face = pltpu.roll(pltpu.roll(value[:, 384:], 64, 1), 1, 0)
        head = value[:, :128] + jnp.where(low_lanes((64, 128)), face, 0.0)
        return jnp.concatenate([head, value[:, 128:]], axis=1)

    share = DT / with_face(jacobian * node_w)
    for f in range(4):
        value = with_face(-change[64 * f : 64 * f + 64] * node_w)
        steps[f] = value * share
        high, low = split(value)
        table[64 * f : 64 * f + 64, :] = high
        table[64 * f + 256 : 64 * f + 320, :] = low
    table[512:528, :] = node_parts[...]
    volumes[0] = jnp.broadcast_to(jacobian, (64, 128))
    volumes[1] = pltpu.roll(volumes[0], 1, 0)

    pick(table, volumes, section[0], section_n[0], send, 0)
    ids = carried(1 - core[0], section, cross, False)
    counts = carried_counts(1 - core[0], section_n, cross_n, False)
    for j in range(3):
        pick(table, volumes, ids[j], counts[j], send, j + 1)


def gather_kernel(table, volumes, section, cross, section_n, cross_n, core, send):
    ids = carried(core[0], section, cross, False)
    counts = carried_counts(core[0], section_n, cross_n, False)
    for j in range(3):
        pick(table, volumes, ids[j], counts[j], send, j)


def pack_kernel(far_a, far_b, far_c, back):
    for j, far in enumerate((far_a, far_b, far_c)):
        back[j] = far[1]


def scatter_kernel(
    steps, section, cross, section_n, cross_n, core, sent, own, shared, far_a, far_b, far_c, total
):
    side = core[0]
    ids = carried(side, section, cross, True)
    counts = carried_counts(side, section_n, cross_n, True)
    added = spread(section[0], section_n[0], sent[0], shared[0])
    mine = (own[0], own[1], sent[3])
    for j, far in enumerate((far_a, far_b, far_c)):
        added += spread(ids[j], counts[j], mine[j], far[0])
    for f in range(4):
        total[f] = steps[f] + added[64 * f : 64 * f + 64]


def update_kernel(
    density, momentum, total, section, cross, section_n, cross_n, core, sent, own, relayed,
    new_density, new_momentum, ready, arrived,
):
    side = 1 - core[0]
    ids = carried(side, section, cross, True)
    counts = carried_counts(side, section_n, cross_n, True)
    mine = (sent[1], sent[2], own[2])
    added = None
    for j in range(3):
        more = spread(ids[j], counts[j], mine[j], relayed[j])
        added = more if added is None else added + more
    lanes = lax.broadcasted_iota(jnp.int32, (64, 128), 1)
    copies = []
    for f in range(4):
        step = total[f] + added[64 * f : 64 * f + 64]
        face = pltpu.roll(pltpu.roll(step[:, :128], 64, 1), 63, 0)
        tail = jnp.where(lanes < 64, step[:, 384:], face)
        step = jnp.concatenate([step[:, :384], tail], axis=1)
        ready[f] = (density[...] if f == 0 else momentum[f - 1]) + step
        target = new_density if f == 0 else new_momentum.at[f - 1]
        copies.append(pltpu.make_async_copy(ready.at[f], target, arrived.at[f]))
        copies[f].start()
    for copy in copies:
        copy.wait()


def relay_pairs(mesh_shape, step):
    groups, members = mesh_shape
    pairs = []
    for g in range(groups):
        for m in range(members):
            core = m % 2
            if step < 2:
                target = (g, m ^ (1 << (2 - step + 2 * core)))
            else:
                target = ((g + 1 - 2 * core) % groups, m)
            pairs.append((g * members + m, target[0] * members + target[1]))
    return pairs


def local(
    density, momentum, element_size, section_slots, section_counts, cross_slots, cross_counts
):
    rho, mom = density[0, 0], momentum[0, 0]
    sizes = element_size.reshape(3, 1, 64)
    slots = section_slots.shape[-1]
    section = section_slots.reshape(5, 1, slots)
    cross = cross_slots[0, 0]
    core = (lax.axis_index("cube") & 1).reshape(1)
    where = (section, cross, section_counts[0, 0], cross_counts[0, 0], core)
    whole = pl.BlockSpec(memory_space=pltpu.VMEM)
    scalars = pl.BlockSpec(memory_space=pltpu.SMEM)
    where_specs = [whole] * 2 + [scalars] * 3
    members = lax.axis_size("cube")
    groups = lax.axis_size("grp")
    near = [(i, i ^ 1) for i in range(members)]

    def on_chip(value):
        return pltpu.with_memory_space_constraint(value, pltpu.VMEM)

    def near_chip(shape, dtype=F32):
        return pltpu.VMEM(shape, dtype)

    steps, table, volumes, sent = pl.pallas_call(
        sums_kernel,
        out_shape=(
            near_chip((4, 64, 512)),
            near_chip((528, 512), BF16),
            near_chip((2, 64, 128)),
            near_chip((4, 5, 8, 128)),
        ),
        in_specs=[whole] * 7 + where_specs,
        out_specs=(whole,) * 4,
        name="sums_and_gather",
    )(rho, mom, sizes, *[jnp.asarray(t) for t in tables()], *where)

    shared = lax.ppermute(sent, "cube", near)
    own = pl.pallas_call(
        gather_kernel,
        out_shape=near_chip((3, 5, 8, 128)),
        in_specs=[whole] * 2 + where_specs,
        out_specs=whole,
        name="gather",
    )(on_chip(table), on_chip(volumes), *where)

    far = [None] * 3
    for step in range(3):
        both = jnp.stack([own[step], shared[step + 1]])
        part = lax.ppermute(both, ("grp", "cube"), relay_pairs((groups, members), step))
        far[step] = on_chip(part)
    back = pl.pallas_call(
        pack_kernel,
        out_shape=near_chip((3, 5, 8, 128)),
        in_specs=[whole] * 3,
        out_specs=whole,
        name="pack",
    )(*far)
    relayed = lax.ppermute(back, "cube", near)
    total = pl.pallas_call(
        scatter_kernel,
        out_shape=near_chip((4, 64, 512)),
        in_specs=[whole] + where_specs + [whole] * 6,
        out_specs=whole,
        name="scatter",
    )(on_chip(steps), *where, on_chip(sent), on_chip(own), on_chip(shared), *far)
    hbm = pl.BlockSpec(memory_space=pl.ANY)
    new_density, new_momentum = pl.pallas_call(
        update_kernel,
        out_shape=(
            jax.ShapeDtypeStruct(rho.shape, F32),
            jax.ShapeDtypeStruct(mom.shape, F32),
        ),
        in_specs=[whole] * 3 + where_specs + [whole] * 3,
        out_specs=(hbm, hbm),
        scratch_shapes=[pltpu.VMEM((4, 64, 512), F32), pltpu.SemaphoreType.DMA((4,))],
        name="scatter_and_update",
    )(on_chip(rho), on_chip(mom), on_chip(total), *where, on_chip(sent), on_chip(own), on_chip(relayed))
    return (new_density[None, None], new_momentum[None, None])


def solution(mesh):
    placed = (
        P("grp", "cube", None, None),
        P("grp", "cube", None, None, None),
        P("grp", "cube", None, None),
        P("grp", "cube", None, None),
        P("grp", "cube", None),
        P("grp", "cube", None, None),
        P("grp", "cube", None),
    )

    return jax.shard_map(
        local,
        mesh=mesh,
        in_specs=placed,
        out_specs=(P("grp", "cube", None, None), P("grp", "cube", None, None, None)),
        check_vma=False,
    )
```

```python
import jax
import jax.numpy as jnp
import numpy as np
from jax import lax
from jax.experimental import pallas as pl
from jax.experimental.pallas import tpu as pltpu
from jax.sharding import PartitionSpec as P

GAMMA = 1.4
DT = 0.01
ORDER = 7
COLS = 448
F32 = jnp.float32
BF16 = jnp.bfloat16


def gll_tables():
    points = np.array(
        [
            -1.0,
            -0.8717401485096066,
            -0.5917001814331423,
            -0.2092992179024789,
            0.2092992179024789,
            0.5917001814331423,
            0.8717401485096066,
            1.0,
        ]
    )
    weights = np.array(
        [
            1.0 / 28.0,
            0.2107042271435061,
            0.3411226924835044,
            0.4124587946587038,
            0.4124587946587038,
            0.3411226924835044,
            0.2107042271435061,
            1.0 / 28.0,
        ]
    )
    previous = np.ones(8)
    current = points.copy()
    for order_now in range(1, ORDER):
        following = ((2 * order_now + 1) * points * current - order_now * previous) / (
            order_now + 1
        )
        previous = current
        current = following
    derivative = np.zeros((8, 8))
    for i in range(8):
        for j in range(8):
            if i != j:
                derivative[i, j] = current[i] / (current[j] * (points[i] - points[j]))
    derivative[0, 0] = -ORDER * (ORDER + 1) / 4.0
    derivative[7, 7] = ORDER * (ORDER + 1) / 4.0
    return (points, weights, derivative)


def bf16_parts(table, count):
    rest = np.asarray(table, np.float32)
    parts = []
    for _ in range(count):
        part = rest.astype(BF16)
        parts.append(part)
        rest = rest - part.astype(np.float32)
    return parts


def tables():
    _, weights, derivative = gll_tables()
    along_second = np.kron(np.eye(4), np.kron(derivative, np.eye(8))).T
    along_third = np.kron(np.eye(32), derivative).T
    first = np.zeros((32, 128), np.float32)
    for t in range(4):
        for s in range(4):
            for r in range(2):
                for half in range(2):
                    factor = derivative[2 * t + half, 2 * s + (half ^ r)]
                    first[8 * t + 2 * s + r, 64 * half : 64 * half + 64] = factor
    inner = np.stack(bf16_parts(along_second, 2) + bf16_parts(along_third, 2))
    node = np.kron(weights, np.kron(weights, weights)).astype(np.float32)[None]
    node_parts = np.concatenate(
        bf16_parts(node, 3) + [np.zeros((13, 512), np.float32).astype(BF16)], axis=0
    )
    return first, inner, node, node_parts


def split(value):
    high = value.astype(BF16)
    low = (value - high.astype(F32)).astype(BF16)
    return high, low


def element_and_column(ids):
    element = lax.shift_right_logical(lax.shift_right_logical(ids, 6) * 9363, 16)
    return element, ids - element * COLS


def column_onehot(column):
    rows = lax.broadcasted_iota(jnp.int32, (512, column.shape[1]), 0)
    return jnp.where(rows == column, 1.0, 0.0).astype(BF16)


def element_mask(element):
    rows = lax.broadcasted_iota(jnp.int32, (64, element.shape[1]), 0)
    return rows == element


def as_column(row):
    shape = (64, 64)
    same = lax.broadcasted_iota(jnp.int32, shape, 0) == lax.broadcasted_iota(jnp.int32, shape, 1)
    return jnp.sum(jnp.where(same, row, 0.0), axis=1, keepdims=True)


def low_lanes(shape):
    return lax.broadcasted_iota(jnp.int32, shape, 1) < 64


def dot(a, b):
    return jnp.dot(a, b, preferred_element_type=F32)


def pick(table, volumes, ids, count, send, at):
    element, column = element_and_column(ids)
    picked = dot(table[...], column_onehot(column))
    mask = element_mask(element)
    live = lax.broadcasted_iota(jnp.int32, ids.shape, 1) < count
    volume = jnp.where(mask, volumes[0, :, :1], 0.0)
    face_volume = jnp.where(jnp.logical_and(mask, column < 64), volumes[1, :, :1], 0.0)
    volume = jnp.sum(volume + face_volume, axis=0, keepdims=True)
    rows = []
    for f in range(4):
        row = picked[64 * f : 64 * f + 64] + picked[64 * f + 256 : 64 * f + 320]
        rows.append(jnp.sum(jnp.where(mask, row, 0.0), axis=0, keepdims=True))
    rows.append(volume * (picked[512:513] + picked[513:514] + picked[514:515]))
    for f in range(5):
        row = jnp.where(live, rows[f], 0.0)
        for t in range(8):
            send[at, f, t : t + 1, :] = row[:, 128 * t : 128 * t + 128]


def spread(ids, count, own, got):
    at = lax.broadcasted_iota(jnp.int32, (8, 128), 0) * 128
    live = at + lax.broadcasted_iota(jnp.int32, (8, 128), 1) < count
    before = DT / own[4]
    after = DT / (own[4] + got[4])
    parts = []
    for f in range(4):
        change = (own[f] + got[f]) * after - own[f] * before
        parts.append(split(jnp.where(live, change, 0.0)))
    element, column = element_and_column(ids)
    mask = element_mask(element)
    rows = []
    for p in range(2):
        for f in range(4):
            part = parts[f][p].astype(F32)
            row = jnp.concatenate([part[t : t + 1, :] for t in range(8)], axis=1)
            rows.append(jnp.where(mask, row, 0.0).astype(BF16))
    added = lax.dot_general(
        jnp.concatenate(rows, axis=0), column_onehot(column), (((1,), (1,)), ((), ())),
        preferred_element_type=F32,
    )
    return added[:256] + added[256:]


def carried(side, section, cross, arriving):
    lower = side == (0 if arriving else 1)
    return [
        section[2 + 2 * side],
        section[1 + 2 * side],
        jnp.where(lower, cross[0:1, :], cross[1:2, :]),
    ]


def carried_counts(side, section_n, cross_n, arriving):
    lower = side == (0 if arriving else 1)
    return [
        section_n[2 + 2 * side],
        section_n[1 + 2 * side],
        jnp.where(lower, cross_n[0], cross_n[1]),
    ]


def sums_kernel(
    density, momentum, sizes, first, inner, node, node_parts, section, cross, section_n, cross_n,
    code, steps, table, volumes, send, far_own, near_own,
):
    rho = density[...]
    inverse = 1.0 / rho
    mom = [momentum[a] for a in range(3)]
    velocity = [m * inverse for m in mom]
    pressure = jnp.exp(GAMMA * jnp.log(rho))
    h = [as_column(sizes[d]) for d in range(3)]
    scale = [h[1] * h[2] * 0.25, h[0] * h[2] * 0.25, h[0] * h[1] * 0.25]
    jacobian = h[0] * h[1] * h[2] * 0.125

    def flux(d):
        parts = [mom[d]]
        for a in range(3):
            part = mom[a] * velocity[d]
            parts.append(part + pressure if a == d else part)
        return [part * scale[d] for part in parts]

    def along_first(part):
        tiles = [part[:, 128 * t : 128 * t + 128] for t in range(4)]
        swapped = [pltpu.roll(tile, 64, 1) for tile in tiles]
        outs = []
        for t in range(4):
            out = None
            for s in range(4):
                for r, tile in enumerate((tiles[s], swapped[s])):
                    at = 8 * t + 2 * s + r
                    term = tile * first[at : at + 1, :]
                    out = term if out is None else out + term
            outs.append(out)
        return jnp.concatenate(outs, axis=1)

    halves = [None, None]
    for d in (1, 2):
        high, low = split(jnp.concatenate(flux(d), axis=0))
        big, small = inner[2 * d - 2], inner[2 * d - 1]
        for k in range(2):
            lanes = slice(256 * k, 256 * k + 256)
            half = dot(high[:, lanes], big) + dot(low[:, lanes], big) + dot(high[:, lanes], small)
            halves[k] = half if halves[k] is None else halves[k] + half
    fluxes = flux(0)
    change = jnp.concatenate(halves, axis=1)
    node_w = node[...]

    def with_face(value):
        face = pltpu.roll(pltpu.roll(value[:, 384:], 64, 1), 1, 0)
        head = value[:, :128] + jnp.where(low_lanes((64, 128)), face, 0.0)
        return jnp.concatenate([head, value[:, 128:]], axis=1)

    share = DT / with_face(jacobian * node_w)
    for f in range(4):
        value = with_face(-(change[64 * f : 64 * f + 64] + along_first(fluxes[f])) * node_w)
        steps[f] = value * share
        high, low = split(value)
        table[64 * f : 64 * f + 64, :] = high
        table[64 * f + 256 : 64 * f + 320, :] = low
    table[512:528, :] = node_parts[...]
    volumes[0] = jnp.broadcast_to(jacobian, (64, 128))
    volumes[1] = pltpu.roll(volumes[0], 1, 0)

    side = code[0] & 1
    ids = carried(1 - side, section, cross, False)
    counts = carried_counts(1 - side, section_n, cross_n, False)
    for j in range(3):
        pick(table, volumes, ids[j], counts[j], send, j)

    @pl.when(code[0] >= 2)
    def _():
        pick_far(table, volumes, section, cross, section_n, cross_n, side, far_own)
        pick_near(table, volumes, section, section_n, side, near_own)


def pick_far(table, volumes, section, cross, section_n, cross_n, side, own):
    ids = carried(side, section, cross, False)[2]
    pick(table, volumes, ids, carried_counts(side, section_n, cross_n, False)[2], own, 0)


def pick_near(table, volumes, section, section_n, side, own):
    for j, at in enumerate((2 + 2 * side, 1 + 2 * side, 0)):
        pick(table, volumes, section[at], section_n[at], own, j)


def far_kernel(table, volumes, section, cross, section_n, cross_n, code, before, own):
    @pl.when(code[0] < 2)
    def _():
        pick_far(table, volumes, section, cross, section_n, cross_n, code[0] & 1, own)


def near_kernel(table, volumes, section, cross, section_n, cross_n, code, before, own):
    @pl.when(code[0] < 2)
    def _():
        pick_near(table, volumes, section, section_n, code[0] & 1, own)


def pack_kernel(far_a, far_b, far_c, own, back):
    for j, far in enumerate((far_a, far_b, far_c)):
        back[j] = far[1]
    back[3] = own[2]


def scatter_kernel(
    steps, section, cross, section_n, cross_n, code, sent, near_own, far_a, far_b, far_c, total
):
    side = code[0] & 1
    ids = carried(side, section, cross, True)
    counts = carried_counts(side, section_n, cross_n, True)
    mine = (near_own[0], near_own[1], sent[2])
    added = None
    for j, far in enumerate((far_a, far_b, far_c)):
        more = spread(ids[j], counts[j], mine[j], far[0])
        added = more if added is None else added + more
    for f in range(4):
        total[f] = steps[f] + added[64 * f : 64 * f + 64]


def update_kernel(
    density, momentum, total, section, cross, section_n, cross_n, code, sent, near_own, far_own,
    relayed, new_density, new_momentum, ready, arrived,
):
    side = 1 - (code[0] & 1)
    ids = carried(side, section, cross, True)
    counts = carried_counts(side, section_n, cross_n, True)
    mine = (sent[0], sent[1], far_own[0])
    added = spread(section[0], section_n[0], near_own[2], relayed[3])
    for j in range(3):
        added += spread(ids[j], counts[j], mine[j], relayed[j])
    lanes = lax.broadcasted_iota(jnp.int32, (64, 128), 1)
    copies = []
    for f in range(4):
        step = total[f] + added[64 * f : 64 * f + 64]
        face = pltpu.roll(pltpu.roll(step[:, :128], 64, 1), 63, 0)
        tail = jnp.where(lanes < 64, step[:, 384:], face)
        step = jnp.concatenate([step[:, :384], tail], axis=1)
        ready[f] = (density[...] if f == 0 else momentum[f - 1]) + step
        target = new_density if f == 0 else new_momentum.at[f - 1]
        copies.append(pltpu.make_async_copy(ready.at[f], target, arrived.at[f]))
        copies[f].start()
    for copy in copies:
        copy.wait()


def relay_pairs(mesh_shape, step):
    groups, members = mesh_shape
    pairs = []
    for g in range(groups):
        for m in range(members):
            core = m % 2
            if step < 2:
                target = (g, m ^ (1 << (2 - step + 2 * core)))
            else:
                target = ((g + 1 - 2 * core) % groups, m)
            pairs.append((g * members + m, target[0] * members + target[1]))
    return pairs


def local(
    density, momentum, element_size, section_slots, section_counts, cross_slots, cross_counts
):
    rho, mom = density[0, 0], momentum[0, 0]
    sizes = element_size.reshape(3, 1, 64)
    slots = section_slots.shape[-1]
    section = section_slots.reshape(5, 1, slots)
    cross = cross_slots[0, 0]
    members = lax.axis_size("cube")
    groups = lax.axis_size("grp")
    device = lax.axis_index("grp") * members + lax.axis_index("cube")
    early = jnp.logical_and(device > 0, device < members)
    code = ((device & 1) + 2 * early.astype(jnp.int32)).reshape(1)
    where = (section, cross, section_counts[0, 0], cross_counts[0, 0], code)
    whole = pl.BlockSpec(memory_space=pltpu.VMEM)
    scalars = pl.BlockSpec(memory_space=pltpu.SMEM)
    where_specs = [whole] * 2 + [scalars] * 3
    near = [(i, i ^ 1) for i in range(members)]

    def on_chip(value):
        return pltpu.with_memory_space_constraint(value, pltpu.VMEM)

    def near_chip(shape, dtype=F32):
        return pltpu.VMEM(shape, dtype)

    section_sums = (5, 8, 128)
    steps, table, volumes, sent, far_own, near_own = pl.pallas_call(
        sums_kernel,
        out_shape=(
            near_chip((4, 64, 512)),
            near_chip((528, 512), BF16),
            near_chip((2, 64, 128)),
            near_chip((3,) + section_sums),
            near_chip((1,) + section_sums),
            near_chip((3,) + section_sums),
        ),
        in_specs=[whole] * 7 + where_specs,
        out_specs=(whole,) * 6,
        name="sums_and_gather",
    )(rho, mom, sizes, *[jnp.asarray(t) for t in tables()], *where)
    shared = lax.ppermute(sent, "cube", near)

    def gather(kernel, own):
        return pl.pallas_call(
            kernel,
            out_shape=near_chip(own.shape),
            in_specs=[whole] * 2 + where_specs + [whole],
            out_specs=whole,
            input_output_aliases={7: 0},
        )(on_chip(table), on_chip(volumes), *where, on_chip(own))

    far_own = gather(far_kernel, far_own)
    near_own = gather(near_kernel, near_own)
    far = [None] * 3
    for step in range(3):
        own = far_own[0] if step == 2 else near_own[step]
        both = jnp.stack([own, shared[step]])
        part = lax.ppermute(both, ("grp", "cube"), relay_pairs((groups, members), step))
        far[step] = on_chip(part)
    back = pl.pallas_call(
        pack_kernel,
        out_shape=near_chip((4,) + section_sums),
        in_specs=[whole] * 4,
        out_specs=whole,
        name="pack",
    )(*far, on_chip(near_own))
    relayed = lax.ppermute(back, "cube", near)
    total = pl.pallas_call(
        scatter_kernel,
        out_shape=near_chip((4, 64, 512)),
        in_specs=[whole] + where_specs + [whole] * 5,
        out_specs=whole,
        name="scatter",
    )(on_chip(steps), *where, on_chip(sent), on_chip(near_own), *far)
    hbm = pl.BlockSpec(memory_space=pl.ANY)
    new_density, new_momentum = pl.pallas_call(
        update_kernel,
        out_shape=(
            jax.ShapeDtypeStruct(rho.shape, F32),
            jax.ShapeDtypeStruct(mom.shape, F32),
        ),
        in_specs=[whole] * 3 + where_specs + [whole] * 4,
        out_specs=(hbm, hbm),
        scratch_shapes=[pltpu.VMEM((4, 64, 512), F32), pltpu.SemaphoreType.DMA((4,))],
        name="scatter_and_update",
    )(
        on_chip(rho), on_chip(mom), on_chip(total), *where, on_chip(sent), on_chip(near_own),
        on_chip(far_own), on_chip(relayed),
    )
    return (new_density[None, None], new_momentum[None, None])


def solution(mesh):
    placed = (
        P("grp", "cube", None, None),
        P("grp", "cube", None, None, None),
        P("grp", "cube", None, None),
        P("grp", "cube", None, None),
        P("grp", "cube", None),
        P("grp", "cube", None, None),
        P("grp", "cube", None),
    )

    return jax.shard_map(
        local,
        mesh=mesh,
        in_specs=placed,
        out_specs=(P("grp", "cube", None, None), P("grp", "cube", None, None, None)),
        check_vma=False,
    )
```

```python
import functools

import jax
import jax.numpy as jnp
import numpy as np
from jax import lax
from jax.experimental import pallas as pl
from jax.experimental.pallas import tpu as pltpu
from jax.sharding import PartitionSpec as P

GAMMA = 1.4
DT = 0.01
ORDER = 7
COLS = 448
F32 = jnp.float32
BF16 = jnp.bfloat16


def gll_tables():
    points = np.array(
        [
            -1.0,
            -0.8717401485096066,
            -0.5917001814331423,
            -0.2092992179024789,
            0.2092992179024789,
            0.5917001814331423,
            0.8717401485096066,
            1.0,
        ]
    )
    weights = np.array(
        [
            1.0 / 28.0,
            0.2107042271435061,
            0.3411226924835044,
            0.4124587946587038,
            0.4124587946587038,
            0.3411226924835044,
            0.2107042271435061,
            1.0 / 28.0,
        ]
    )
    previous = np.ones(8)
    current = points.copy()
    for order_now in range(1, ORDER):
        following = ((2 * order_now + 1) * points * current - order_now * previous) / (
            order_now + 1
        )
        previous = current
        current = following
    derivative = np.zeros((8, 8))
    for i in range(8):
        for j in range(8):
            if i != j:
                derivative[i, j] = current[i] / (current[j] * (points[i] - points[j]))
    derivative[0, 0] = -ORDER * (ORDER + 1) / 4.0
    derivative[7, 7] = ORDER * (ORDER + 1) / 4.0
    return (points, weights, derivative)


def bf16_parts(table, count):
    rest = np.asarray(table, np.float32)
    parts = []
    for _ in range(count):
        part = rest.astype(BF16)
        parts.append(part)
        rest = rest - part.astype(np.float32)
    return parts


def tables():
    _, weights, derivative = gll_tables()
    along_second = np.kron(np.eye(4), np.kron(derivative, np.eye(8))).T
    along_third = np.kron(np.eye(32), derivative).T
    first = np.zeros((32, 128), np.float32)
    for t in range(4):
        for s in range(4):
            for r in range(2):
                for half in range(2):
                    factor = derivative[2 * t + half, 2 * s + (half ^ r)]
                    first[8 * t + 2 * s + r, 64 * half : 64 * half + 64] = factor
    inner = np.stack(bf16_parts(along_second, 2) + bf16_parts(along_third, 2))
    node = np.kron(weights, np.kron(weights, weights)).astype(np.float32)[None]
    node_parts = np.concatenate(
        bf16_parts(node, 3) + [np.zeros((13, 512), np.float32).astype(BF16)], axis=0
    )
    return first, inner, node, node_parts


def split(value):
    high = value.astype(BF16)
    low = (value - high.astype(F32)).astype(BF16)
    return high, low


def element_and_column(ids):
    element = lax.shift_right_logical(lax.shift_right_logical(ids, 6) * 9363, 16)
    return element, ids - element * COLS


def column_onehot(column):
    rows = lax.broadcasted_iota(jnp.int32, (512, column.shape[1]), 0)
    return jnp.where(rows == column, 1.0, 0.0).astype(BF16)


def element_mask(element):
    rows = lax.broadcasted_iota(jnp.int32, (64, element.shape[1]), 0)
    return rows == element


def as_column(row):
    shape = (64, 64)
    same = lax.broadcasted_iota(jnp.int32, shape, 0) == lax.broadcasted_iota(jnp.int32, shape, 1)
    return jnp.sum(jnp.where(same, row, 0.0), axis=1, keepdims=True)


def low_lanes(shape):
    return lax.broadcasted_iota(jnp.int32, shape, 1) < 64


def dot(a, b):
    return jnp.dot(a, b, preferred_element_type=F32)


def pick(table, volumes, ids, count, send, at):
    element, column = element_and_column(ids)
    picked = dot(table[...], column_onehot(column))
    mask = element_mask(element)
    limit = jnp.concatenate([count[:1, :]] * 8, axis=1)
    live = lax.broadcasted_iota(jnp.int32, ids.shape, 1) < limit
    volume = jnp.where(mask, volumes[0, :, :1], 0.0)
    face_volume = jnp.where(jnp.logical_and(mask, column < 64), volumes[1, :, :1], 0.0)
    volume = jnp.sum(volume + face_volume, axis=0, keepdims=True)
    rows = []
    for f in range(4):
        row = picked[64 * f : 64 * f + 64] + picked[64 * f + 256 : 64 * f + 320]
        rows.append(jnp.sum(jnp.where(mask, row, 0.0), axis=0, keepdims=True))
    rows.append(volume * (picked[512:513] + picked[513:514] + picked[514:515]))
    for f in range(5):
        row = jnp.where(live, rows[f], 0.0)
        for t in range(8):
            send[at, f, t : t + 1, :] = row[:, 128 * t : 128 * t + 128]


def spread(ids, count, own, got):
    at = lax.broadcasted_iota(jnp.int32, (8, 128), 0) * 128
    live = at + lax.broadcasted_iota(jnp.int32, (8, 128), 1) < count
    before = DT / own[4]
    after = DT / (own[4] + got[4])
    parts = []
    for f in range(4):
        change = (own[f] + got[f]) * after - own[f] * before
        parts.append(split(jnp.where(live, change, 0.0)))
    element, column = element_and_column(ids)
    mask = element_mask(element)
    rows = []
    for p in range(2):
        for f in range(4):
            part = parts[f][p].astype(F32)
            row = jnp.concatenate([part[t : t + 1, :] for t in range(8)], axis=1)
            rows.append(jnp.where(mask, row, 0.0).astype(BF16))
    added = lax.dot_general(
        jnp.concatenate(rows, axis=0), column_onehot(column), (((1,), (1,)), ((), ())),
        preferred_element_type=F32,
    )
    return added[:256] + added[256:]


NEAR = (0, 1, 3)
FAR = 2
OTHERS = (4, 5, 6)
ARRIVING = (0, 1, 6)
RELAYED = (4, 5, 2, 3)


def make_plan(section, cross, section_n, cross_n, code, ids, counts):
    side = code[0] & 1
    for row, core in ((0, side), (4, 1 - side)):
        for j in range(2):
            at = 2 - j + 2 * core
            ids[row + j] = section[at]
            counts[row + j] = jnp.full((8, 128), section_n[at], jnp.int32)
        upper = core == 0
        ids[row + 2 if row == 4 else FAR] = jnp.where(upper, cross[1:2, :], cross[0:1, :])
        limit = jnp.where(upper, cross_n[1], cross_n[0])
        counts[row + 2 if row == 4 else FAR] = jnp.full((8, 128), limit, jnp.int32)
    ids[3] = section[0]
    counts[3] = jnp.full((8, 128), section_n[0], jnp.int32)
    counts[7] = jnp.full((8, 128), code[0], jnp.int32)


def sums_kernel(
    density, momentum, sizes, first, inner, node, node_parts, section, cross, section_n, cross_n,
    code, steps, table, volumes, send, far_own, near_own, ids, counts,
):
    rho = density[...]
    inverse = 1.0 / rho
    mom = [momentum[a] for a in range(3)]
    velocity = [m * inverse for m in mom]
    pressure = jnp.exp(GAMMA * jnp.log(rho))
    h = [as_column(sizes[d]) for d in range(3)]
    scale = [h[1] * h[2] * 0.25, h[0] * h[2] * 0.25, h[0] * h[1] * 0.25]
    jacobian = h[0] * h[1] * h[2] * 0.125

    def flux(d):
        parts = [mom[d]]
        for a in range(3):
            part = mom[a] * velocity[d]
            parts.append(part + pressure if a == d else part)
        return [part * scale[d] for part in parts]

    def along_first(part):
        tiles = [part[:, 128 * t : 128 * t + 128] for t in range(4)]
        swapped = [pltpu.roll(tile, 64, 1) for tile in tiles]
        outs = []
        for t in range(4):
            out = None
            for s in range(4):
                for r, tile in enumerate((tiles[s], swapped[s])):
                    at = 8 * t + 2 * s + r
                    term = tile * first[at : at + 1, :]
                    out = term if out is None else out + term
            outs.append(out)
        return jnp.concatenate(outs, axis=1)

    halves = [None, None]
    for d in (1, 2):
        high, low = split(jnp.concatenate(flux(d), axis=0))
        big, small = inner[2 * d - 2], inner[2 * d - 1]
        for k in range(2):
            lanes = slice(256 * k, 256 * k + 256)
            half = dot(high[:, lanes], big) + dot(low[:, lanes], big) + dot(high[:, lanes], small)
            halves[k] = half if halves[k] is None else halves[k] + half
    fluxes = flux(0)
    change = jnp.concatenate(halves, axis=1)
    node_w = node[...]

    def with_face(value):
        face = pltpu.roll(pltpu.roll(value[:, 384:], 64, 1), 1, 0)
        head = value[:, :128] + jnp.where(low_lanes((64, 128)), face, 0.0)
        return jnp.concatenate([head, value[:, 128:]], axis=1)

    share = DT / with_face(jacobian * node_w)
    for f in range(4):
        value = with_face(-(change[64 * f : 64 * f + 64] + along_first(fluxes[f])) * node_w)
        steps[f] = value * share
        high, low = split(value)
        table[64 * f : 64 * f + 64, :] = high
        table[64 * f + 256 : 64 * f + 320, :] = low
    table[512:528, :] = node_parts[...]
    volumes[0] = jnp.broadcast_to(jacobian, (64, 128))
    volumes[1] = pltpu.roll(volumes[0], 1, 0)

    make_plan(section, cross, section_n, cross_n, code, ids, counts)
    for j, row in enumerate(OTHERS):
        pick(table, volumes, ids[row], counts[row], send, j)

    @pl.when(code[0] >= 2)
    def _():
        pick(table, volumes, ids[FAR], counts[FAR], far_own, 0)
        for j, row in enumerate(NEAR):
            pick(table, volumes, ids[row], counts[row], near_own, j)


def late_kernel(rows, table, volumes, ids, counts, before, own):
    @pl.when(jnp.max(counts[7]) < 2)
    def _():
        for j, row in enumerate(rows):
            pick(table, volumes, ids[row], counts[row], own, j)


def pack_kernel(far_a, far_b, far_c, own, back):
    for j, far in enumerate((far_a, far_b, far_c)):
        back[j] = far[1]
    back[3] = own[2]


def scatter_kernel(way, steps, ids, counts, mine, far, total):
    row = ARRIVING[way]
    added = spread(ids[row], counts[row], mine[way], far[0])
    for f in range(4):
        total[f] = steps[f] + added[64 * f : 64 * f + 64]


def update_kernel(
    density, momentum, total, ids, counts, sent, near_own, far_own, relayed, new_density,
    new_momentum, ready, arrived,
):
    mine = (sent[0], sent[1], far_own[0], near_own[2])
    added = None
    for j, row in enumerate(RELAYED):
        more = spread(ids[row], counts[row], mine[j], relayed[j])
        added = more if added is None else added + more
    lanes = lax.broadcasted_iota(jnp.int32, (64, 128), 1)
    copies = []
    for f in range(4):
        step = total[f] + added[64 * f : 64 * f + 64]
        face = pltpu.roll(pltpu.roll(step[:, :128], 64, 1), 63, 0)
        tail = jnp.where(lanes < 64, step[:, 384:], face)
        step = jnp.concatenate([step[:, :384], tail], axis=1)
        ready[f] = (density[...] if f == 0 else momentum[f - 1]) + step
        target = new_density if f == 0 else new_momentum.at[f - 1]
        copies.append(pltpu.make_async_copy(ready.at[f], target, arrived.at[f]))
        copies[f].start()
    for copy in copies:
        copy.wait()


def relay_pairs(mesh_shape, step):
    groups, members = mesh_shape
    pairs = []
    for g in range(groups):
        for m in range(members):
            core = m % 2
            if step < 2:
                target = (g, m ^ (1 << (2 - step + 2 * core)))
            else:
                target = ((g + 1 - 2 * core) % groups, m)
            pairs.append((g * members + m, target[0] * members + target[1]))
    return pairs


def local(
    density, momentum, element_size, section_slots, section_counts, cross_slots, cross_counts
):
    rho, mom = density[0, 0], momentum[0, 0]
    sizes = element_size.reshape(3, 1, 64)
    slots = section_slots.shape[-1]
    section = section_slots.reshape(5, 1, slots)
    cross = cross_slots[0, 0]
    members = lax.axis_size("cube")
    groups = lax.axis_size("grp")
    device = lax.axis_index("grp") * members + lax.axis_index("cube")
    early = jnp.logical_and(device > 0, device < members)
    code = ((device & 1) + 2 * early.astype(jnp.int32)).reshape(1)
    whole = pl.BlockSpec(memory_space=pltpu.VMEM)
    scalars = pl.BlockSpec(memory_space=pltpu.SMEM)
    near = [(i, i ^ 1) for i in range(members)]

    def on_chip(value):
        return pltpu.with_memory_space_constraint(value, pltpu.VMEM)

    def near_chip(shape, dtype=F32):
        return pltpu.VMEM(shape, dtype)

    section_sums = (5, 8, 128)
    steps, table, volumes, sent, far_own, near_own, ids, counts = pl.pallas_call(
        sums_kernel,
        out_shape=(
            near_chip((4, 64, 512)),
            near_chip((528, 512), BF16),
            near_chip((2, 64, 128)),
            near_chip((3,) + section_sums),
            near_chip((1,) + section_sums),
            near_chip((3,) + section_sums),
            near_chip((7, 1, slots), jnp.int32),
            near_chip((8, 8, 128), jnp.int32),
        ),
        in_specs=[whole] * 9 + [scalars] * 3,
        out_specs=(whole,) * 8,
        name="sums_and_gather",
    )(
        rho, mom, sizes, *[jnp.asarray(t) for t in tables()], section, cross,
        section_counts[0, 0], cross_counts[0, 0], code,
    )
    plan = (on_chip(ids), on_chip(counts))
    shared = lax.ppermute(sent, "cube", near)

    def gather(rows, own):
        return pl.pallas_call(
            functools.partial(late_kernel, rows),
            out_shape=near_chip(own.shape),
            in_specs=[whole] * 5,
            out_specs=whole,
            input_output_aliases={4: 0},
        )(on_chip(table), on_chip(volumes), *plan, on_chip(own))

    far_own = gather((FAR,), far_own)
    near_own = gather(NEAR, near_own)
    far = [None] * 3
    for step in range(3):
        own = far_own[0] if step == 2 else near_own[step]
        both = jnp.stack([own, shared[step]])
        part = lax.ppermute(both, ("grp", "cube"), relay_pairs((groups, members), step))
        far[step] = on_chip(part)
    back = pl.pallas_call(
        pack_kernel,
        out_shape=near_chip((4,) + section_sums),
        in_specs=[whole] * 4,
        out_specs=whole,
        name="pack",
    )(*far, on_chip(near_own))
    relayed = lax.ppermute(back, "cube", near)
    total = steps
    for way in (2, 0, 1):
        total = pl.pallas_call(
            functools.partial(scatter_kernel, way),
            out_shape=near_chip((4, 64, 512)),
            in_specs=[whole] * 5,
            out_specs=whole,
            input_output_aliases={0: 0},
        )(on_chip(total), *plan, on_chip(sent if way == 2 else near_own), far[way])
    hbm = pl.BlockSpec(memory_space=pl.ANY)
    new_density, new_momentum = pl.pallas_call(
        update_kernel,
        out_shape=(
            jax.ShapeDtypeStruct(rho.shape, F32),
            jax.ShapeDtypeStruct(mom.shape, F32),
        ),
        in_specs=[whole] * 9,
        out_specs=(hbm, hbm),
        scratch_shapes=[pltpu.VMEM((4, 64, 512), F32), pltpu.SemaphoreType.DMA((4,))],
        name="scatter_and_update",
    )(
        on_chip(rho), on_chip(mom), on_chip(total), *plan, on_chip(sent), on_chip(near_own),
        on_chip(far_own), on_chip(relayed),
    )
    return (new_density[None, None], new_momentum[None, None])


def solution(mesh):
    placed = (
        P("grp", "cube", None, None),
        P("grp", "cube", None, None, None),
        P("grp", "cube", None, None),
        P("grp", "cube", None, None),
        P("grp", "cube", None),
        P("grp", "cube", None, None),
        P("grp", "cube", None),
    )

    return jax.shard_map(
        local,
        mesh=mesh,
        in_specs=placed,
        out_specs=(P("grp", "cube", None, None), P("grp", "cube", None, None, None)),
        check_vma=False,
    )
```

```python
import functools

import jax
import jax.numpy as jnp
import numpy as np
from jax import lax
from jax.experimental import pallas as pl
from jax.experimental.pallas import tpu as pltpu
from jax.sharding import PartitionSpec as P

GAMMA = 1.4
DT = 0.01
ORDER = 7
COLS = 448
F32 = jnp.float32
BF16 = jnp.bfloat16


def gll_tables():
    points = np.array(
        [
            -1.0,
            -0.8717401485096066,
            -0.5917001814331423,
            -0.2092992179024789,
            0.2092992179024789,
            0.5917001814331423,
            0.8717401485096066,
            1.0,
        ]
    )
    weights = np.array(
        [
            1.0 / 28.0,
            0.2107042271435061,
            0.3411226924835044,
            0.4124587946587038,
            0.4124587946587038,
            0.3411226924835044,
            0.2107042271435061,
            1.0 / 28.0,
        ]
    )
    previous = np.ones(8)
    current = points.copy()
    for order_now in range(1, ORDER):
        following = ((2 * order_now + 1) * points * current - order_now * previous) / (
            order_now + 1
        )
        previous = current
        current = following
    derivative = np.zeros((8, 8))
    for i in range(8):
        for j in range(8):
            if i != j:
                derivative[i, j] = current[i] / (current[j] * (points[i] - points[j]))
    derivative[0, 0] = -ORDER * (ORDER + 1) / 4.0
    derivative[7, 7] = ORDER * (ORDER + 1) / 4.0
    return (points, weights, derivative)


def bf16_parts(table, count):
    rest = np.asarray(table, np.float32)
    parts = []
    for _ in range(count):
        part = rest.astype(BF16)
        parts.append(part)
        rest = rest - part.astype(np.float32)
    return parts


def tables():
    _, weights, derivative = gll_tables()
    along_second = np.kron(np.eye(4), np.kron(derivative, np.eye(8))).T
    along_third = np.kron(np.eye(32), derivative).T
    first = np.zeros((16, 128), np.float32)
    for p in range(2):
        for t in range(2):
            for s in range(2):
                for r in range(2):
                    for half in range(2):
                        a, c = 2 * t + half, 2 * s + (half ^ r)
                        factor = derivative[a, c] + (-1) ** p * derivative[a, 7 - c]
                        row = 8 * p + 4 * t + 2 * s + r
                        first[row, 64 * half : 64 * half + 64] = factor / 2
    inner = []
    for table in (along_second, along_third):
        big, small = bf16_parts(table, 2)
        inner += [big, big, small]
    inner = np.concatenate(inner, axis=0)
    node = np.kron(weights, np.kron(weights, weights)).astype(np.float32)[None]
    node_parts = np.concatenate(
        bf16_parts(node, 3) + [np.zeros((13, 512), np.float32).astype(BF16)], axis=0
    )
    return first, inner, node, node_parts


def split(value):
    high = value.astype(BF16)
    low = (value - high.astype(F32)).astype(BF16)
    return high, low


def element_and_column(ids):
    element = lax.shift_right_logical(lax.shift_right_logical(ids, 6) * 9363, 16)
    return element, ids - element * COLS


def column_onehot(column):
    rows = lax.broadcasted_iota(jnp.int32, (512, column.shape[1]), 0)
    return jnp.where(rows == column, 1.0, 0.0).astype(BF16)


def element_mask(element):
    rows = lax.broadcasted_iota(jnp.int32, (64, element.shape[1]), 0)
    return rows == element


def as_column(row):
    shape = (64, 64)
    same = lax.broadcasted_iota(jnp.int32, shape, 0) == lax.broadcasted_iota(jnp.int32, shape, 1)
    return jnp.sum(jnp.where(same, row, 0.0), axis=1, keepdims=True)


def low_lanes(shape):
    return lax.broadcasted_iota(jnp.int32, shape, 1) < 64


def dot(a, b):
    return jnp.dot(a, b, preferred_element_type=F32)


def pick(table, volumes, ids, count, send, at):
    element, column = element_and_column(ids)
    picked = dot(table[...], column_onehot(column))
    mask = element_mask(element)
    limit = jnp.concatenate([count[:1, :]] * 8, axis=1)
    live = lax.broadcasted_iota(jnp.int32, ids.shape, 1) < limit
    volume = jnp.where(mask, volumes[0, :, :1], 0.0)
    face_volume = jnp.where(jnp.logical_and(mask, column < 64), volumes[1, :, :1], 0.0)
    volume = jnp.sum(volume + face_volume, axis=0, keepdims=True)
    rows = []
    for f in range(4):
        row = picked[64 * f : 64 * f + 64] + picked[64 * f + 256 : 64 * f + 320]
        rows.append(jnp.sum(jnp.where(mask, row, 0.0), axis=0, keepdims=True))
    rows.append(volume * (picked[512:513] + picked[513:514] + picked[514:515]))
    for f in range(5):
        row = jnp.where(live, rows[f], 0.0)
        for t in range(8):
            send[at, f, t : t + 1, :] = row[:, 128 * t : 128 * t + 128]


def spread(ids, count, own, got):
    at = lax.broadcasted_iota(jnp.int32, (8, 128), 0) * 128
    live = at + lax.broadcasted_iota(jnp.int32, (8, 128), 1) < count
    before = DT / own[4]
    after = DT / (own[4] + got[4])
    parts = []
    for f in range(4):
        change = (own[f] + got[f]) * after - own[f] * before
        parts.append(split(jnp.where(live, change, 0.0)))
    element, column = element_and_column(ids)
    mask = element_mask(element)
    rows = []
    for p in range(2):
        for f in range(4):
            part = parts[f][p].astype(F32)
            row = jnp.concatenate([part[t : t + 1, :] for t in range(8)], axis=1)
            rows.append(jnp.where(mask, row, 0.0).astype(BF16))
    added = lax.dot_general(
        jnp.concatenate(rows, axis=0), column_onehot(column), (((1,), (1,)), ((), ())),
        preferred_element_type=F32,
    )
    return added[:256] + added[256:]


NEAR = (0, 1, 3)
FAR = 2
OTHERS = (4, 5, 6)
ARRIVING = (0, 1, 6)
RELAYED = (4, 5, 2, 3)


def make_plan(section, cross, section_n, cross_n, code, ids, counts):
    side = code[0] & 1
    for row, core in ((0, side), (4, 1 - side)):
        for j in range(2):
            at = 2 - j + 2 * core
            ids[row + j] = section[at]
            counts[row + j] = jnp.full((8, 128), section_n[at], jnp.int32)
        upper = core == 0
        ids[row + 2 if row == 4 else FAR] = jnp.where(upper, cross[1:2, :], cross[0:1, :])
        limit = jnp.where(upper, cross_n[1], cross_n[0])
        counts[row + 2 if row == 4 else FAR] = jnp.full((8, 128), limit, jnp.int32)
    ids[3] = section[0]
    counts[3] = jnp.full((8, 128), section_n[0], jnp.int32)
    counts[7] = jnp.full((8, 128), code[0], jnp.int32)


def sums_kernel(
    density, momentum, sizes, first, inner, node, node_parts, section, cross, section_n, cross_n,
    code, steps, table, volumes, send, far_own, near_own, ids, counts,
):
    rho = density[...]
    inverse = 1.0 / rho
    mom = [momentum[a] for a in range(3)]
    velocity = [m * inverse for m in mom]
    pressure = jnp.exp(GAMMA * jnp.log(rho))
    h = [as_column(sizes[d]) for d in range(3)]
    scale = [h[1] * h[2] * 0.25, h[0] * h[2] * 0.25, h[0] * h[1] * 0.25]
    jacobian = h[0] * h[1] * h[2] * 0.125

    def flux(d):
        parts = [mom[d]]
        for a in range(3):
            part = mom[a] * velocity[d]
            parts.append(part + pressure if a == d else part)
        return [part * scale[d] for part in parts]

    def along_first(part):
        tiles = [part[:, 128 * t : 128 * t + 128] for t in range(4)]
        mirror = [pltpu.roll(tiles[3 - t], 64, 1) for t in range(2)]
        outs = []
        for p in range(2):
            halves = [tiles[t] - mirror[t] if p else tiles[t] + mirror[t] for t in range(2)]
            swapped = [pltpu.roll(half, 64, 1) for half in halves]
            outs.append([])
            for t in range(2):
                out = None
                for s in range(2):
                    for r, tile in enumerate((halves[s], swapped[s])):
                        at = 8 * p + 4 * t + 2 * s + r
                        term = tile * first[at : at + 1, :]
                        out = term if out is None else out + term
                outs[p].append(out)
        head = [outs[0][t] + outs[1][t] for t in range(2)]
        tail = [pltpu.roll(outs[1][t] - outs[0][t], 64, 1) for t in range(2)]
        return jnp.concatenate(head + tail[::-1], axis=1)

    parts = [split(jnp.concatenate(flux(d), axis=0)) for d in (1, 2)]
    halves = []
    for k in range(2):
        lanes = slice(256 * k, 256 * k + 256)
        deep = [part[:, lanes] for high, low in parts for part in (high, low, high)]
        halves.append(dot(jnp.concatenate(deep, axis=1), inner[...]))
    fluxes = flux(0)
    change = jnp.concatenate(halves, axis=1)
    node_w = node[...]

    def with_face(value):
        face = pltpu.roll(pltpu.roll(value[:, 384:], 64, 1), 1, 0)
        head = value[:, :128] + jnp.where(low_lanes((64, 128)), face, 0.0)
        return jnp.concatenate([head, value[:, 128:]], axis=1)

    share = DT / with_face(jacobian * node_w)
    for f in range(4):
        value = with_face(-(change[64 * f : 64 * f + 64] + along_first(fluxes[f])) * node_w)
        steps[f] = value * share
        high, low = split(value)
        table[64 * f : 64 * f + 64, :] = high
        table[64 * f + 256 : 64 * f + 320, :] = low
    table[512:528, :] = node_parts[...]
    volumes[0] = jnp.broadcast_to(jacobian, (64, 128))
    volumes[1] = pltpu.roll(volumes[0], 1, 0)

    make_plan(section, cross, section_n, cross_n, code, ids, counts)
    for j, row in enumerate(OTHERS):
        pick(table, volumes, ids[row], counts[row], send, j)

    @pl.when(code[0] >= 2)
    def _():
        pick(table, volumes, ids[FAR], counts[FAR], far_own, 0)
        for j, row in enumerate(NEAR):
            pick(table, volumes, ids[row], counts[row], near_own, j)


def late_kernel(rows, table, volumes, ids, counts, before, own):
    @pl.when(jnp.max(counts[7]) < 2)
    def _():
        for j, row in enumerate(rows):
            pick(table, volumes, ids[row], counts[row], own, j)


def pack_kernel(far_a, far_b, far_c, own, back):
    for j, far in enumerate((far_a, far_b, far_c)):
        back[j] = far[1]
    back[3] = own[2]


def scatter_kernel(ways, steps, ids, counts, sent, near_own, *fars_and_total):
    fars, total = fars_and_total[:-1], fars_and_total[-1]
    added = None
    for way, far in zip(ways, fars):
        row = ARRIVING[way]
        mine = sent[2] if way == 2 else near_own[way]
        more = spread(ids[row], counts[row], mine, far[0])
        added = more if added is None else added + more
    for f in range(4):
        total[f] = steps[f] + added[64 * f : 64 * f + 64]


def update_kernel(
    density, momentum, total, ids, counts, sent, near_own, far_own, relayed, new_density,
    new_momentum, ready, arrived,
):
    mine = (sent[0], sent[1], far_own[0], near_own[2])
    added = None
    for j, row in enumerate(RELAYED):
        more = spread(ids[row], counts[row], mine[j], relayed[j])
        added = more if added is None else added + more
    lanes = lax.broadcasted_iota(jnp.int32, (64, 128), 1)
    copies = []
    for f in range(4):
        step = total[f] + added[64 * f : 64 * f + 64]
        face = pltpu.roll(pltpu.roll(step[:, :128], 64, 1), 63, 0)
        tail = jnp.where(lanes < 64, step[:, 384:], face)
        step = jnp.concatenate([step[:, :384], tail], axis=1)
        ready[f] = (density[...] if f == 0 else momentum[f - 1]) + step
        target = new_density if f == 0 else new_momentum.at[f - 1]
        copies.append(pltpu.make_async_copy(ready.at[f], target, arrived.at[f]))
        copies[f].start()
    for copy in copies:
        copy.wait()


def relay_pairs(mesh_shape, step):
    groups, members = mesh_shape
    pairs = []
    for g in range(groups):
        for m in range(members):
            core = m % 2
            if step < 2:
                target = (g, m ^ (1 << (2 - step + 2 * core)))
            else:
                target = ((g + 1 - 2 * core) % groups, m)
            pairs.append((g * members + m, target[0] * members + target[1]))
    return pairs


def local(
    density, momentum, element_size, section_slots, section_counts, cross_slots, cross_counts
):
    rho, mom = density[0, 0], momentum[0, 0]
    sizes = element_size.reshape(3, 1, 64)
    slots = section_slots.shape[-1]
    section = section_slots.reshape(5, 1, slots)
    cross = cross_slots[0, 0]
    members = lax.axis_size("cube")
    groups = lax.axis_size("grp")
    device = lax.axis_index("grp") * members + lax.axis_index("cube")
    early = jnp.logical_and(device > 0, device < members)
    code = ((device & 1) + 2 * early.astype(jnp.int32)).reshape(1)
    whole = pl.BlockSpec(memory_space=pltpu.VMEM)
    scalars = pl.BlockSpec(memory_space=pltpu.SMEM)
    near = [(i, i ^ 1) for i in range(members)]

    def on_chip(value):
        return pltpu.with_memory_space_constraint(value, pltpu.VMEM)

    def near_chip(shape, dtype=F32):
        return pltpu.VMEM(shape, dtype)

    section_sums = (5, 8, 128)
    steps, table, volumes, sent, far_own, near_own, ids, counts = pl.pallas_call(
        sums_kernel,
        out_shape=(
            near_chip((4, 64, 512)),
            near_chip((528, 512), BF16),
            near_chip((2, 64, 128)),
            near_chip((3,) + section_sums),
            near_chip((1,) + section_sums),
            near_chip((3,) + section_sums),
            near_chip((7, 1, slots), jnp.int32),
            near_chip((8, 8, 128), jnp.int32),
        ),
        in_specs=[whole] * 9 + [scalars] * 3,
        out_specs=(whole,) * 8,
        name="sums_and_gather",
    )(
        rho, mom, sizes, *[jnp.asarray(t) for t in tables()], section, cross,
        section_counts[0, 0], cross_counts[0, 0], code,
    )
    plan = (on_chip(ids), on_chip(counts))
    shared = lax.ppermute(sent, "cube", near)

    def gather(rows, own):
        return pl.pallas_call(
            functools.partial(late_kernel, rows),
            out_shape=near_chip(own.shape),
            in_specs=[whole] * 5,
            out_specs=whole,
            input_output_aliases={4: 0},
        )(on_chip(table), on_chip(volumes), *plan, on_chip(own))

    far_own = gather((FAR,), far_own)
    near_own = gather(NEAR, near_own)
    far = [None] * 3
    for step in range(3):
        own = far_own[0] if step == 2 else near_own[step]
        both = jnp.stack([own, shared[step]])
        part = lax.ppermute(both, ("grp", "cube"), relay_pairs((groups, members), step))
        far[step] = on_chip(part)
    back = pl.pallas_call(
        pack_kernel,
        out_shape=near_chip((4,) + section_sums),
        in_specs=[whole] * 4,
        out_specs=whole,
        name="pack",
    )(*far, on_chip(near_own))
    relayed = lax.ppermute(back, "cube", near)
    total = steps
    for ways in ((2, 0), (1,)):
        total = pl.pallas_call(
            functools.partial(scatter_kernel, ways),
            out_shape=near_chip((4, 64, 512)),
            in_specs=[whole] * (5 + len(ways)),
            out_specs=whole,
            input_output_aliases={0: 0},
        )(
            on_chip(total), *plan, on_chip(sent), on_chip(near_own),
            *[far[way] for way in ways],
        )
    hbm = pl.BlockSpec(memory_space=pl.ANY)
    new_density, new_momentum = pl.pallas_call(
        update_kernel,
        out_shape=(
            jax.ShapeDtypeStruct(rho.shape, F32),
            jax.ShapeDtypeStruct(mom.shape, F32),
        ),
        in_specs=[whole] * 9,
        out_specs=(hbm, hbm),
        scratch_shapes=[pltpu.VMEM((4, 64, 512), F32), pltpu.SemaphoreType.DMA((4,))],
        name="scatter_and_update",
    )(
        on_chip(rho), on_chip(mom), on_chip(total), *plan, on_chip(sent), on_chip(near_own),
        on_chip(far_own), on_chip(relayed),
    )
    return (new_density[None, None], new_momentum[None, None])


def solution(mesh):
    placed = (
        P("grp", "cube", None, None),
        P("grp", "cube", None, None, None),
        P("grp", "cube", None, None),
        P("grp", "cube", None, None),
        P("grp", "cube", None),
        P("grp", "cube", None, None),
        P("grp", "cube", None),
    )

    return jax.shard_map(
        local,
        mesh=mesh,
        in_specs=placed,
        out_specs=(P("grp", "cube", None, None), P("grp", "cube", None, None, None)),
        check_vma=False,
    )
```

```python
import functools

import jax
import jax.numpy as jnp
import numpy as np
from jax import lax
from jax.experimental import pallas as pl
from jax.experimental.pallas import tpu as pltpu
from jax.sharding import PartitionSpec as P

GAMMA = 1.4
DT = 0.01
ORDER = 7
COLS = 448
F32 = jnp.float32
BF16 = jnp.bfloat16


def gll_tables():
    points = np.array(
        [
            -1.0,
            -0.8717401485096066,
            -0.5917001814331423,
            -0.2092992179024789,
            0.2092992179024789,
            0.5917001814331423,
            0.8717401485096066,
            1.0,
        ]
    )
    weights = np.array(
        [
            1.0 / 28.0,
            0.2107042271435061,
            0.3411226924835044,
            0.4124587946587038,
            0.4124587946587038,
            0.3411226924835044,
            0.2107042271435061,
            1.0 / 28.0,
        ]
    )
    previous = np.ones(8)
    current = points.copy()
    for order_now in range(1, ORDER):
        following = ((2 * order_now + 1) * points * current - order_now * previous) / (
            order_now + 1
        )
        previous = current
        current = following
    derivative = np.zeros((8, 8))
    for i in range(8):
        for j in range(8):
            if i != j:
                derivative[i, j] = current[i] / (current[j] * (points[i] - points[j]))
    derivative[0, 0] = -ORDER * (ORDER + 1) / 4.0
    derivative[7, 7] = ORDER * (ORDER + 1) / 4.0
    return (points, weights, derivative)


def bf16_parts(table, count):
    rest = np.asarray(table, np.float32)
    parts = []
    for _ in range(count):
        part = rest.astype(BF16)
        parts.append(part)
        rest = rest - part.astype(np.float32)
    return parts


def tables():
    _, weights, derivative = gll_tables()
    along_second = np.kron(np.eye(4), np.kron(derivative, np.eye(8))).T
    along_third = np.kron(np.eye(32), derivative).T
    first = np.zeros((16, 128), np.float32)
    for p in range(2):
        for t in range(2):
            for s in range(2):
                for r in range(2):
                    for half in range(2):
                        a, c = 2 * t + half, 2 * s + (half ^ r)
                        factor = derivative[a, c] + (-1) ** p * derivative[a, 7 - c]
                        row = 8 * p + 4 * t + 2 * s + r
                        first[row, 64 * half : 64 * half + 64] = factor / 2
    inner = []
    for table in (along_second, along_third):
        big, small = bf16_parts(table, 2)
        inner += [big, big, small]
    inner = np.concatenate(inner, axis=0)
    node = np.kron(weights, np.kron(weights, weights)).astype(np.float32)[None]
    node_parts = np.concatenate(
        bf16_parts(node, 3) + [np.zeros((13, 512), np.float32).astype(BF16)], axis=0
    )
    return first, inner, node, node_parts


def split(value):
    high = value.astype(BF16)
    low = (value - high.astype(F32)).astype(BF16)
    return high, low


def element_and_column(ids):
    element = lax.shift_right_logical(lax.shift_right_logical(ids, 6) * 9363, 16)
    return element, ids - element * COLS


def column_onehot(column):
    rows = lax.broadcasted_iota(jnp.int32, (512, column.shape[1]), 0)
    return jnp.where(rows == column, 1.0, 0.0).astype(BF16)


def element_mask(element):
    rows = lax.broadcasted_iota(jnp.int32, (64, element.shape[1]), 0)
    return rows == element


def as_column(row):
    shape = (64, 64)
    same = lax.broadcasted_iota(jnp.int32, shape, 0) == lax.broadcasted_iota(jnp.int32, shape, 1)
    return jnp.sum(jnp.where(same, row, 0.0), axis=1, keepdims=True)


def low_lanes(shape):
    return lax.broadcasted_iota(jnp.int32, shape, 1) < 64


def dot(a, b):
    return jnp.dot(a, b, preferred_element_type=F32)


def pick(table, volumes, ids, count, send, at):
    element, column = element_and_column(ids)
    picked = dot(table[...], column_onehot(column))
    mask = element_mask(element)
    limit = jnp.concatenate([count[:1, :]] * 8, axis=1)
    live = lax.broadcasted_iota(jnp.int32, ids.shape, 1) < limit
    volume = jnp.where(mask, volumes[0, :, :1], 0.0)
    face_volume = jnp.where(jnp.logical_and(mask, column < 64), volumes[1, :, :1], 0.0)
    volume = jnp.sum(volume + face_volume, axis=0, keepdims=True)
    rows = []
    for f in range(4):
        row = picked[64 * f : 64 * f + 64] + picked[64 * f + 256 : 64 * f + 320]
        rows.append(jnp.sum(jnp.where(mask, row, 0.0), axis=0, keepdims=True))
    rows.append(volume * (picked[512:513] + picked[513:514] + picked[514:515]))
    for f in range(5):
        row = jnp.where(live, rows[f], 0.0)
        for t in range(8):
            send[at, f, t : t + 1, :] = row[:, 128 * t : 128 * t + 128]


def spread(ids, count, own, got):
    at = lax.broadcasted_iota(jnp.int32, (8, 128), 0) * 128
    live = at + lax.broadcasted_iota(jnp.int32, (8, 128), 1) < count
    before = DT / own[4]
    after = DT / (own[4] + got[4])
    parts = []
    for f in range(4):
        change = (own[f] + got[f]) * after - own[f] * before
        parts.append(split(jnp.where(live, change, 0.0)))
    element, column = element_and_column(ids)
    mask = element_mask(element)
    rows = []
    for p in range(2):
        for f in range(4):
            part = parts[f][p].astype(F32)
            row = jnp.concatenate([part[t : t + 1, :] for t in range(8)], axis=1)
            rows.append(jnp.where(mask, row, 0.0).astype(BF16))
    added = lax.dot_general(
        jnp.concatenate(rows, axis=0), column_onehot(column), (((1,), (1,)), ((), ())),
        preferred_element_type=F32,
    )
    return added[:256] + added[256:]


NEAR = (0, 1, 3)
FAR = 2
OTHERS = (4, 5, 6)
ARRIVING = (0, 1, 6)
RELAYED = (4, 5, 2, 3)


def make_plan(section, cross, section_n, cross_n, code, ids, counts):
    side = code[0] & 1
    for row, core in ((0, side), (4, 1 - side)):
        for j in range(2):
            at = 2 - j + 2 * core
            ids[row + j] = section[at]
            counts[row + j] = jnp.full((8, 128), section_n[at], jnp.int32)
        upper = core == 0
        ids[row + 2 if row == 4 else FAR] = jnp.where(upper, cross[1:2, :], cross[0:1, :])
        limit = jnp.where(upper, cross_n[1], cross_n[0])
        counts[row + 2 if row == 4 else FAR] = jnp.full((8, 128), limit, jnp.int32)
    ids[3] = section[0]
    counts[3] = jnp.full((8, 128), section_n[0], jnp.int32)
    counts[7] = jnp.full((8, 128), code[0], jnp.int32)


def sums_kernel(
    density, momentum, sizes, first, inner, node, node_parts, section, cross, section_n, cross_n,
    code, steps, table, volumes, send, far_own, near_own, ids, counts,
):
    rho = density[...]
    inverse = 1.0 / rho
    mom = [momentum[a] for a in range(3)]
    velocity = [m * inverse for m in mom]
    pressure = jnp.exp(GAMMA * jnp.log(rho))
    h = [as_column(sizes[d]) for d in range(3)]
    scale = [h[1] * h[2] * 0.25, h[0] * h[2] * 0.25, h[0] * h[1] * 0.25]
    jacobian = h[0] * h[1] * h[2] * 0.125

    def flux(d):
        parts = [mom[d]]
        for a in range(3):
            part = mom[a] * velocity[d]
            parts.append(part + pressure if a == d else part)
        return [part * scale[d] for part in parts]

    def along_first(part):
        tiles = [part[:, 128 * t : 128 * t + 128] for t in range(4)]
        mirror = [pltpu.roll(tiles[3 - t], 64, 1) for t in range(2)]
        outs = []
        for p in range(2):
            halves = [tiles[t] - mirror[t] if p else tiles[t] + mirror[t] for t in range(2)]
            swapped = [pltpu.roll(half, 64, 1) for half in halves]
            outs.append([])
            for t in range(2):
                out = None
                for s in range(2):
                    for r, tile in enumerate((halves[s], swapped[s])):
                        at = 8 * p + 4 * t + 2 * s + r
                        term = tile * first[at : at + 1, :]
                        out = term if out is None else out + term
                outs[p].append(out)
        head = [outs[0][t] + outs[1][t] for t in range(2)]
        tail = [pltpu.roll(outs[1][t] - outs[0][t], 64, 1) for t in range(2)]
        return jnp.concatenate(head + tail[::-1], axis=1)

    parts = [split(jnp.concatenate(flux(d), axis=0)) for d in (1, 2)]
    halves = []
    for k in range(2):
        lanes = slice(256 * k, 256 * k + 256)
        deep = [part[:, lanes] for high, low in parts for part in (high, low, high)]
        halves.append(dot(jnp.concatenate(deep, axis=1), inner[...]))
    fluxes = flux(0)
    change = jnp.concatenate(halves, axis=1)
    node_w = node[...]

    def with_face(value):
        face = pltpu.roll(pltpu.roll(value[:, 384:], 64, 1), 1, 0)
        head = value[:, :128] + jnp.where(low_lanes((64, 128)), face, 0.0)
        return jnp.concatenate([head, value[:, 128:]], axis=1)

    share = DT / with_face(jacobian * node_w)
    for f in range(4):
        value = with_face(-(change[64 * f : 64 * f + 64] + along_first(fluxes[f])) * node_w)
        steps[f] = value * share
        high, low = split(value)
        table[64 * f : 64 * f + 64, :] = high
        table[64 * f + 256 : 64 * f + 320, :] = low
    table[512:528, :] = node_parts[...]
    volumes[0] = jnp.broadcast_to(jacobian, (64, 128))
    volumes[1] = pltpu.roll(volumes[0], 1, 0)

    make_plan(section, cross, section_n, cross_n, code, ids, counts)
    pick(table, volumes, ids[OTHERS[2]], counts[OTHERS[2]], send, 2)

    @pl.when(code[0] < 4)
    def _():
        for j in range(2):
            pick(table, volumes, ids[OTHERS[j]], counts[OTHERS[j]], send, j)

    @pl.when(code[0] >= 4)
    def _():
        for j in range(2):
            send[j] = jnp.zeros((5, 8, 128), F32)

    @pl.when(code[0] & 2 == 2)
    def _():
        pick(table, volumes, ids[FAR], counts[FAR], far_own, 0)
        for j, row in enumerate(NEAR):
            pick(table, volumes, ids[row], counts[row], near_own, j)


def far_kernel(table, volumes, ids, counts, before, own):
    @pl.when(jnp.max(counts[7]) & 2 == 0)
    def _():
        pick(table, volumes, ids[FAR], counts[FAR], own, 0)


def near_kernel(table, volumes, ids, counts, before, own, rest):
    code = jnp.max(counts[7])

    @pl.when(code & 2 == 0)
    def _():
        for j, row in enumerate(NEAR):
            pick(table, volumes, ids[row], counts[row], own, j)

    @pl.when(code >= 4)
    def _():
        for j in range(2):
            pick(table, volumes, ids[OTHERS[j]], counts[OTHERS[j]], rest, j)

    @pl.when(code < 4)
    def _():
        for j in range(2):
            rest[j] = jnp.zeros((5, 8, 128), F32)


def pack_far_kernel(own, shared, both):
    both[0] = own[0]
    both[1] = shared[2]


def pack_near_kernel(own, shared, late_shared, *both):
    for j in range(2):
        both[j][0] = own[j]
        both[j][1] = shared[j] + late_shared[j]


def pack_kernel(far_a, far_b, far_c, own, back):
    for j, far in enumerate((far_a, far_b, far_c)):
        back[j] = far[1]
    back[3] = own[2]


def scatter_kernel(ways, steps, ids, counts, sent, near_own, *fars_and_total):
    fars, total = fars_and_total[:-1], fars_and_total[-1]
    added = None
    for way, far in zip(ways, fars):
        row = ARRIVING[way]
        mine = sent[2] if way == 2 else near_own[way]
        more = spread(ids[row], counts[row], mine, far[0])
        added = more if added is None else added + more
    for f in range(4):
        total[f] = steps[f] + added[64 * f : 64 * f + 64]


def update_kernel(
    density, momentum, total, ids, counts, sent, rest, near_own, far_own, relayed, new_density,
    new_momentum, ready, arrived,
):
    mine = (sent[0] + rest[0], sent[1] + rest[1], far_own[0], near_own[2])
    added = None
    for j, row in enumerate(RELAYED):
        more = spread(ids[row], counts[row], mine[j], relayed[j])
        added = more if added is None else added + more
    lanes = lax.broadcasted_iota(jnp.int32, (64, 128), 1)
    copies = []
    for f in range(4):
        step = total[f] + added[64 * f : 64 * f + 64]
        face = pltpu.roll(pltpu.roll(step[:, :128], 64, 1), 63, 0)
        tail = jnp.where(lanes < 64, step[:, 384:], face)
        step = jnp.concatenate([step[:, :384], tail], axis=1)
        ready[f] = (density[...] if f == 0 else momentum[f - 1]) + step
        target = new_density if f == 0 else new_momentum.at[f - 1]
        copies.append(pltpu.make_async_copy(ready.at[f], target, arrived.at[f]))
        copies[f].start()
    for copy in copies:
        copy.wait()


def relay_pairs(mesh_shape, step):
    groups, members = mesh_shape
    pairs = []
    for g in range(groups):
        for m in range(members):
            core = m % 2
            if step < 2:
                target = (g, m ^ (1 << (2 - step + 2 * core)))
            else:
                target = ((g + 1 - 2 * core) % groups, m)
            pairs.append((g * members + m, target[0] * members + target[1]))
    return pairs


def local(
    density, momentum, element_size, section_slots, section_counts, cross_slots, cross_counts
):
    rho, mom = density[0, 0], momentum[0, 0]
    sizes = element_size.reshape(3, 1, 64)
    slots = section_slots.shape[-1]
    section = section_slots.reshape(5, 1, slots)
    cross = cross_slots[0, 0]
    members = lax.axis_size("cube")
    groups = lax.axis_size("grp")
    device = lax.axis_index("grp") * members + lax.axis_index("cube")
    early = jnp.logical_and(device > 0, device < members)
    late = device >= (groups - 1) * members
    code = ((device & 1) + jnp.where(early, 2, jnp.where(late, 4, 0))).reshape(1)
    whole = pl.BlockSpec(memory_space=pltpu.VMEM)
    scalars = pl.BlockSpec(memory_space=pltpu.SMEM)
    near = [(i, i ^ 1) for i in range(members)]

    def on_chip(value):
        return pltpu.with_memory_space_constraint(value, pltpu.VMEM)

    def near_chip(shape, dtype=F32):
        return pltpu.VMEM(shape, dtype)

    section_sums = (5, 8, 128)
    steps, table, volumes, sent, far_own, near_own, ids, counts = pl.pallas_call(
        sums_kernel,
        out_shape=(
            near_chip((4, 64, 512)),
            near_chip((528, 512), BF16),
            near_chip((2, 64, 128)),
            near_chip((3,) + section_sums),
            near_chip((1,) + section_sums),
            near_chip((3,) + section_sums),
            near_chip((7, 1, slots), jnp.int32),
            near_chip((8, 8, 128), jnp.int32),
        ),
        in_specs=[whole] * 9 + [scalars] * 3,
        out_specs=(whole,) * 8,
        name="sums_and_gather",
    )(
        rho, mom, sizes, *[jnp.asarray(t) for t in tables()], section, cross,
        section_counts[0, 0], cross_counts[0, 0], code,
    )
    plan = (on_chip(ids), on_chip(counts))
    shared = lax.ppermute(sent, "cube", near)

    def gather(kernel, own, *more):
        return pl.pallas_call(
            kernel,
            out_shape=(near_chip(own.shape),) + more,
            in_specs=[whole] * 5,
            out_specs=(whole,) * (1 + len(more)),
            input_output_aliases={4: 0},
        )(on_chip(table), on_chip(volumes), *plan, on_chip(own))

    (far_own,) = gather(far_kernel, far_own)
    near_own, rest = gather(near_kernel, near_own, near_chip((2,) + section_sums))
    last = (groups - 1) * members
    late_shared = lax.ppermute(
        rest, ("grp", "cube"), [(last + m, last + (m ^ 1)) for m in range(members)]
    )
    pair = near_chip((2,) + section_sums)
    far_both = pl.pallas_call(
        pack_far_kernel,
        out_shape=pair,
        in_specs=[whole] * 2,
        out_specs=whole,
        name="pack_far",
    )(on_chip(far_own), on_chip(shared))
    near_both = pl.pallas_call(
        pack_near_kernel,
        out_shape=(pair, pair),
        in_specs=[whole] * 3,
        out_specs=(whole, whole),
        name="pack_near",
    )(on_chip(near_own), on_chip(shared), on_chip(late_shared))
    far = []
    for step, both in enumerate((*near_both, far_both)):
        part = lax.ppermute(both, ("grp", "cube"), relay_pairs((groups, members), step))
        far.append(on_chip(part))
    back = pl.pallas_call(
        pack_kernel,
        out_shape=near_chip((4,) + section_sums),
        in_specs=[whole] * 4,
        out_specs=whole,
        name="pack",
    )(*far, on_chip(near_own))
    relayed = lax.ppermute(back, "cube", near)
    total = steps
    for ways in ((2, 0), (1,)):
        total = pl.pallas_call(
            functools.partial(scatter_kernel, ways),
            out_shape=near_chip((4, 64, 512)),
            in_specs=[whole] * (5 + len(ways)),
            out_specs=whole,
            input_output_aliases={0: 0},
        )(
            on_chip(total), *plan, on_chip(sent), on_chip(near_own),
            *[far[way] for way in ways],
        )
    hbm = pl.BlockSpec(memory_space=pl.ANY)
    new_density, new_momentum = pl.pallas_call(
        update_kernel,
        out_shape=(
            jax.ShapeDtypeStruct(rho.shape, F32),
            jax.ShapeDtypeStruct(mom.shape, F32),
        ),
        in_specs=[whole] * 10,
        out_specs=(hbm, hbm),
        scratch_shapes=[pltpu.VMEM((4, 64, 512), F32), pltpu.SemaphoreType.DMA((4,))],
        name="scatter_and_update",
    )(
        on_chip(rho), on_chip(mom), on_chip(total), *plan, on_chip(sent), on_chip(rest),
        on_chip(near_own), on_chip(far_own), on_chip(relayed),
    )
    return (new_density[None, None], new_momentum[None, None])


def solution(mesh):
    placed = (
        P("grp", "cube", None, None),
        P("grp", "cube", None, None, None),
        P("grp", "cube", None, None),
        P("grp", "cube", None, None),
        P("grp", "cube", None),
        P("grp", "cube", None, None),
        P("grp", "cube", None),
    )

    return jax.shard_map(
        local,
        mesh=mesh,
        in_specs=placed,
        out_specs=(P("grp", "cube", None, None), P("grp", "cube", None, None, None)),
        check_vma=False,
    )
```
